128 devices in a mesh: gx: 8 (over y, x_lo), gy: 16 (over z, x_hi, core).
Axes of the slice: x: 4 (x_hi: 2, x_lo: 2; x = x_hi * 2 + x_lo), y: 4, z: 4, core: 2. Of those that a mesh axis runs over, the one named last changes fastest.
Arguments:
- pressure: float32 [192, 384, 256], P('gx', 'gy'), may hold values from -6 to 6
- pressure_old: float32 [192, 384, 256], P('gx', 'gy'), may hold values from -6 to 6
- speed_term: float32 [192, 384, 256], P('gx', 'gy'), may hold values from 0.03 to 0.15
- layer_width: int32 [4], replicated, may hold values from 8 to 16
- source_x: int32 [4], replicated, may hold values from 0 to 191
- source_y: int32 [4], replicated, may hold values from 0 to 383
- source_z: int32 [4], replicated, may hold values from 0 to 255
- source_amp: float32 [8, 4], replicated, may hold values from -8 to 8
- receiver_x: int32 [64], replicated, may hold values from 0 to 191
- receiver_y: int32 [64], replicated, may hold values from 0 to 383
- receiver_z: int32 [64], replicated, may hold values from 0 to 255
Outputs:
- pressure_final: float32 [192, 384, 256], P('gx', 'gy')
- traces: float32 [64, 8], replicated
- energy: float32 [8], replicated
The draws below stay inside these ranges and needn't reach their ends.
All inputs are finite; a program needn't handle non-finite values.
Results may differ from the reference program's by a relative error of at most 0.00026.
Values sent between devices are 32-bit elements; how exact they have to be, the bound alone decides.
No kernel may reach another device: no remote copies, remote signals or barrier semaphores. Data moves between devices by JAX's collectives and lax.ppermute only.
A program may use at most 64 MiB of HBM per device.

```python
import math
import jax
import jax.numpy as jnp
from jax import lax

NZ = 256
STEPS = 8
NSRC = 4
NREC = 64
NX = 192
NY = 384


def plant(entries, key, smallest, largest):
    longest = entries.shape.index(max(entries.shape))
    spots = []
    for shift in (0, 1):
        where = [jax.random.randint(jax.random.fold_in(key, axis), (), 0, length) for axis, length in enumerate(entries.shape)]
        where[longest] = (where[longest] + shift) % entries.shape[longest]
        spots.append(tuple(where))
    return entries.at[spots[0]].set(smallest).at[spots[1]].set(largest)


def block_scale(stream_key, extent, shards, least, top_value):
    level = 1.0
    for dim, shards_of in shards:
        heights = jax.random.uniform(jax.random.fold_in(jax.random.fold_in(stream_key, 6), dim), (shards_of,), jnp.float32, least / len(shards), top_value / len(shards))
        level = level * jnp.repeat(jnp.exp(heights), extent[dim] // shards_of).reshape((-1,) + (1,) * (len(extent) - 1 - dim))
    return level


def centred(stream_key, shape, spread, limit, pieces=(), held_as=jnp.bfloat16):
    drawn = jax.random.normal(stream_key, shape, jnp.float32) * spread
    if len(pieces) > 0:
        drawn = block_scale(stream_key, shape, pieces, -0.22, 0.18) * drawn
    return jnp.clip(drawn, min=-limit, max=limit).astype(held_as)


def setup_inputs(seed: int = 0) -> dict:
    arg_keys = jax.random.split(jax.random.key(seed), 12)
    return {
        "pressure": centred(arg_keys[0], (NX, NY, NZ), 1.0, 6.0, ((0, 8), (1, 16)), jnp.float32),
        "pressure_old": centred(arg_keys[1], (NX, NY, NZ), 1.0, 6.0, ((0, 8), (1, 16)), jnp.float32),
        "speed_term": jnp.clip(jnp.exp(math.log(0.15) - 1.609438 * jax.random.uniform(arg_keys[2], (NX, NY, NZ), jnp.float32) ** block_scale(arg_keys[2], (NX, NY, NZ), ((0, 8), (1, 16)), -0.2, 0.2)), 0.03, 0.15),
        "layer_width": plant(jax.random.randint(arg_keys[3], (4,), 8, 17), jax.random.fold_in(arg_keys[3], 1), 8, 16).astype(jnp.int32),
        "source_x": plant(jax.random.randint(arg_keys[4], (NSRC,), 0, NX), jax.random.fold_in(arg_keys[4], 1), 0, NX - 1).astype(jnp.int32),
        "source_y": plant(jax.random.randint(arg_keys[5], (NSRC,), 0, NY), jax.random.fold_in(arg_keys[5], 1), 0, NY - 1).astype(jnp.int32),
        "source_z": plant(jax.random.randint(arg_keys[6], (NSRC,), 0, NZ), jax.random.fold_in(arg_keys[6], 1), 0, NZ - 1).astype(jnp.int32),
        "source_amp": centred(arg_keys[7], (STEPS, NSRC), 2.0, 8.0, (), jnp.float32),
        "receiver_x": plant(jax.random.randint(arg_keys[8], (NREC,), 0, NX), jax.random.fold_in(arg_keys[8], 1), 0, NX - 1).astype(jnp.int32),
        "receiver_y": plant(jax.random.randint(arg_keys[9], (NREC,), 0, NY), jax.random.fold_in(arg_keys[9], 1), 0, NY - 1).astype(jnp.int32),
        "receiver_z": plant(jax.random.randint(arg_keys[10], (NREC,), 0, NZ), jax.random.fold_in(arg_keys[10], 1), 0, NZ - 1).astype(jnp.int32),
    }


first_coef = (0.8, -0.2, 4.0 / 105.0, -1.0 / 280.0)
second_coef = (1.6, -0.2, 8.0 / 315.0, -1.0 / 560.0)
centre_coef = -205.0 / 72.0
damping = 0.6
radius = 4


def shifted(padded, axis_id, offset, length):
    return lax.slice_in_dim(padded, radius + offset, radius + offset + length, axis=axis_id)


def first_diff(padded, axis_id, length):
    summed = first_coef[0] * (shifted(padded, axis_id, 1, length) - shifted(padded, axis_id, -1, length))
    for shift_by in range(2, 5):
        summed = summed + first_coef[shift_by - 1] * (shifted(padded, axis_id, shift_by, length) - shifted(padded, axis_id, -shift_by, length))
    return summed


def second_diff(padded, axis_id, length):
    summed = centre_coef * shifted(padded, axis_id, 0, length)
    for shift_by in range(1, 5):
        summed = summed + second_coef[shift_by - 1] * (shifted(padded, axis_id, shift_by, length) + shifted(padded, axis_id, -shift_by, length))
    return summed


def profile(position, low_width, high_width, length):
    inward_low = jnp.clip((low_width - position) / low_width, 0.0, 1.0)
    inward_high = jnp.clip((position - (length - 1 - high_width)) / high_width, 0.0, 1.0)
    return jnp.exp(-damping * (inward_low * inward_low + inward_high * inward_high))


def pad_axis(field, axis_id):
    widths = [(0, 0), (0, 0), (0, 0)]
    widths[axis_id] = (radius, radius)
    return jnp.pad(field, widths)


def reference(pressure, pressure_old, speed_term, layer_width, source_x, source_y, source_z, source_amp, receiver_x, receiver_y, receiver_z):
    widths = layer_width.astype(jnp.float32)
    global_x = profile(jnp.arange(NX, dtype=jnp.int32).astype(jnp.float32), widths[0], widths[1], NX)
    global_y = profile(jnp.arange(NY, dtype=jnp.int32).astype(jnp.float32), widths[2], widths[3], NY)
    keep_x = global_x[:, None, None]
    take_x = keep_x - 1.0
    keep_y = global_y[None, :, None]
    take_y = keep_y - 1.0
    weight = 1.0 - keep_x * keep_y
    normaliser = NZ * (float(NX * NY) - jnp.sum(global_x) * jnp.sum(global_y))
    current = pressure
    previous = pressure_old
    memory_x = jnp.zeros_like(pressure)
    memory_y = jnp.zeros_like(pressure)
    zeta_x = jnp.zeros_like(pressure)
    zeta_y = jnp.zeros_like(pressure)
    energies = []
    traces = []
    for step_index in range(STEPS):
        pad_x = pad_axis(current, 0)
        pad_y = pad_axis(current, 1)
        pad_z = pad_axis(current, 2)
        grad_x = first_diff(pad_x, 0, NX)
        grad_y = first_diff(pad_y, 1, NY)
        bend_x = second_diff(pad_x, 0, NX) + first_diff(pad_axis(memory_x, 0), 0, NX)
        zeta_x = keep_x * zeta_x + take_x * bend_x
        bend_y = second_diff(pad_y, 1, NY) + first_diff(pad_axis(memory_y, 1), 1, NY)
        zeta_y = keep_y * zeta_y + take_y * bend_y
        laplace = bend_x + zeta_x + bend_y + zeta_y + second_diff(pad_z, 2, NZ)
        following = 2.0 * current - previous + speed_term * laplace
        following = following.at[source_x, source_y, source_z].add(source_amp[step_index])
        memory_x = keep_x * memory_x + take_x * grad_x
        memory_y = keep_y * memory_y + take_y * grad_y
        energies.append(jnp.sum(weight * following * following) / normaliser)
        traces.append(following[receiver_x, receiver_y, receiver_z])
        previous = current
        current = following
    return current, jnp.stack(traces, axis=1), jnp.stack(energies)
```

```python
import functools

import jax
import jax.numpy as jnp
import ml_dtypes
import numpy as np
from jax import lax
from jax.experimental import pallas as pl
from jax.experimental.pallas import tpu as pltpu
from jax.sharding import PartitionSpec as P

STEPS = 8
NSRC = 4
NREC = 64
NX = 192
NY = 384
NZ = 256
CX = 24
CY = 24
H = 4
LO = 8
LANES = 128
GX = "gx"
GY = "gy"
BOTH = (GX, GY)

first_coef = (0.8, -0.2, 4.0 / 105.0, -1.0 / 280.0)
second_coef = (1.6, -0.2, 8.0 / 315.0, -1.0 / 560.0)
centre_coef = -205.0 / 72.0
damping = 0.6

FIELD = (CX + 2 * H, 2, CY + 2 * LO, LANES)
MEM_X = (CX + 2 * H, 2, CY, LANES)
MEM_Y = (CX, 2, CY + 2 * LO, LANES)
BLOCK = (CX, 2, CY, LANES)
STRIP_X = (H, 2, CY, LANES)
STRIP_Y = (CX, 2, H, LANES)
SEEN = (2 * STEPS, LANES)


def band_matrix():
    band = np.zeros((NZ, NZ), np.float64)
    for i in range(NZ):
        band[i, i] = centre_coef
        for k in range(1, 5):
            if i + k < NZ:
                band[i + k, i] = second_coef[k - 1]
            if i - k >= 0:
                band[i - k, i] = second_coef[k - 1]
    high = band.astype(ml_dtypes.bfloat16)
    low = (band - high.astype(np.float64)).astype(ml_dtypes.bfloat16)
    return np.concatenate([high, high, low], axis=0)


def profile(position, low_width, high_width, length):
    inward_low = jnp.clip((low_width - position) / low_width, 0.0, 1.0)
    inward_high = jnp.clip((position - (length - 1 - high_width)) / high_width, 0.0, 1.0)
    return jnp.exp(-damping * (inward_low * inward_low + inward_high * inward_high))


def wide(value):
    return jnp.full((1, LANES), value, jnp.float32)


def keep_of_row(widths_ref, start_x, i):
    position = (start_x + i).astype(jnp.float32)
    low, high = (widths_ref[0].astype(jnp.float32), widths_ref[1].astype(jnp.float32))
    return profile(wide(position), wide(low), wide(high), NX)


def keep_of_columns(widths_ref, start_y):
    position = (start_y + lax.broadcasted_iota(jnp.int32, (CY, LANES), 0)).astype(jnp.float32)
    low, high = (widths_ref[2].astype(jnp.float32), widths_ref[3].astype(jnp.float32))
    return profile(position, wide(low), wide(high), NY)


def whole_sum(low_width, high_width, length):
    rows = length // LANES + (1 if length % LANES else 0)
    index = lax.broadcasted_iota(jnp.int32, (rows, LANES), 0) * LANES
    index = index + lax.broadcasted_iota(jnp.int32, (rows, LANES), 1)
    low, high = (wide(low_width.astype(jnp.float32)), wide(high_width.astype(jnp.float32)))
    value = profile(index.astype(jnp.float32), low, high, length)
    return jnp.sum(jnp.where(index < length, value, 0.0))


def place():
    gx, gy = (lax.axis_index(GX), lax.axis_index(GY))
    edge_x = (gx == 0) | (gx == lax.axis_size(GX) - 1)
    edge_y = (gy == 0) | (gy == lax.axis_size(GY) - 1)
    return gx, gy, edge_x, edge_y


def observe(field, seen, step, widths_ref, rx, ry, rz):
    gx, gy, edge_x, edge_y = place()
    start_x, start_y = (gx * CX, gy * CY)

    @pl.when(edge_x | edge_y)
    def _():
        keep_y = keep_of_columns(widths_ref, start_y)

        def add_row(i, total):
            weight = 1.0 - keep_of_row(widths_ref, start_x, i) * keep_y
            value = field[i + H, :, LO : LO + CY, :]
            return total + weight * (value[0] * value[0] + value[1] * value[1])

        total = lax.fori_loop(0, CX, add_row, jnp.zeros((CY, LANES), jnp.float32))
        sum_x = whole_sum(widths_ref[0], widths_ref[1], NX)
        sum_y = whole_sum(widths_ref[2], widths_ref[3], NY)
        normaliser = wide(float(NZ) * (float(NX * NY) - sum_x * sum_y))
        seen[STEPS + step : STEPS + step + 1, :] = jnp.sum(total, axis=0, keepdims=True) / normaliser

    lane = lax.broadcasted_iota(jnp.int32, (1, LANES), 1)

    def sample(r, carry):
        lx, ly, z = (rx[r] - start_x, ry[r] - start_y, rz[r])

        @pl.when((lx >= 0) & (lx < CX) & (ly >= 0) & (ly < CY))
        def _():
            line = field[lx + H, z >> 7, pl.ds(ly + LO, 1), :]
            turned = pltpu.roll(line, (r - (z & 127)) & 127, axis=1)
            seen[step : step + 1, :] = jnp.where(lane == r, turned, seen[step : step + 1, :])

        return carry

    lax.fori_loop(0, NREC, sample, 0)


def pack_kernel(pressure, field, up_x, down_x, up_y, down_y):
    field[...] = jnp.zeros(FIELD, jnp.float32)
    for half in range(2):
        part = pressure[:, :, half * LANES : (half + 1) * LANES]
        field[H : H + CX, half, LO : LO + CY, :] = part
    up_x[...] = field[CX : CX + H, :, LO : LO + CY, :]
    down_x[...] = field[H : 2 * H, :, LO : LO + CY, :]
    up_y[...] = field[H : H + CX, :, LO + CY - H : LO + CY, :]
    down_y[...] = field[H : H + CX, :, LO : LO + H, :]


def begin_kernel(old, speed_term, field, speed, memory_x, memory_y, zeta_x, zeta_y, seen):
    field[...] = jnp.zeros(FIELD, jnp.float32)
    for half in range(2):
        lanes = slice(half * LANES, (half + 1) * LANES)
        field[H : H + CX, half, LO : LO + CY, :] = old[:, :, lanes]
        speed[:, half, :, :] = speed_term[:, :, lanes]
    memory_x[...] = jnp.zeros(MEM_X, jnp.float32)
    memory_y[...] = jnp.zeros(MEM_Y, jnp.float32)
    zeta_x[...] = jnp.zeros(BLOCK, jnp.float32)
    zeta_y[...] = jnp.zeros(BLOCK, jnp.float32)
    seen[...] = jnp.zeros(SEEN, jnp.float32)


def inner_kernel(
    step,
    widths_ref,
    sx,
    sy,
    sz,
    amp,
    rx,
    ry,
    rz,
    band,
    current,
    speed,
    previous_in,
    memory_x_in,
    memory_y_in,
    zeta_x_in,
    zeta_y_in,
    seen_in,
    following,
    memory_x,
    memory_y,
    zeta_x,
    zeta_y,
    seen,
    bend_z,
):
    gx, gy, edge_x, edge_y = place()
    start_x, start_y = (gx * CX, gy * CY)
    halves = [current[H : H + CX, h, LO : LO + CY, :].reshape(CX * CY, LANES) for h in range(2)]
    whole = jnp.concatenate(halves, axis=1)
    high = whole.astype(jnp.bfloat16)
    low = (whole - high.astype(jnp.float32)).astype(jnp.bfloat16)
    bent = jnp.dot(
        jnp.concatenate([high, low, high], axis=1), band[...], preferred_element_type=jnp.float32
    )
    for h in range(2):
        bend_z[:, h, :, :] = bent[:, h * LANES : (h + 1) * LANES].reshape(CX, CY, LANES)

    def second_x(i):
        total = centre_coef * current[i + H, :, LO : LO + CY, :]
        for k in range(1, 5):
            pair = current[i + H + k, :, LO : LO + CY, :] + current[i + H - k, :, LO : LO + CY, :]
            total = total + second_coef[k - 1] * pair
        return total

    def second_y(i):
        total = centre_coef * current[i + H, :, LO : LO + CY, :]
        for k in range(1, 5):
            pair = current[i + H, :, LO + k : LO + CY + k, :]
            pair = pair + current[i + H, :, LO - k : LO + CY - k, :]
            total = total + second_coef[k - 1] * pair
        return total

    def first_x(ref, i, lo):
        total = 0.0
        for k in range(1, 5):
            pair = ref[i + H + k, :, lo : lo + CY, :] - ref[i + H - k, :, lo : lo + CY, :]
            total = total + first_coef[k - 1] * pair
        return total

    def first_y(ref, i, off):
        total = 0.0
        for k in range(1, 5):
            pair = ref[i + off, :, LO + k : LO + CY + k, :]
            pair = pair - ref[i + off, :, LO - k : LO + CY - k, :]
            total = total + first_coef[k - 1] * pair
        return total

    def plain(i, carry):
        laplace = second_x(i) + second_y(i) + bend_z[i]
        value = 2.0 * current[i + H, :, LO : LO + CY, :] - previous_in[i + H, :, LO : LO + CY, :]
        following[i + H, :, LO : LO + CY, :] = value + speed[i] * laplace
        return carry

    lax.fori_loop(0, CX, plain, 0)

    @pl.when(edge_x)
    def _():
        def layer(i, carry):
            keep = keep_of_row(widths_ref, start_x, i)[None]
            flux = first_x(memory_x_in, i, 0)
            bend = second_x(i) + flux
            zeta = keep * zeta_x_in[i] + (keep - 1.0) * bend
            zeta_x[i] = zeta
            inside = slice(LO, LO + CY)
            following[i + H, :, inside, :] = following[i + H, :, inside, :] + speed[i] * (flux + zeta)
            return carry

        lax.fori_loop(0, CX, layer, 0)

        def keep_memory(i, carry):
            keep = keep_of_row(widths_ref, start_x, i)[None]
            grad = first_x(current, i, LO)
            memory_x[i + H] = keep * memory_x_in[i + H] + (keep - 1.0) * grad
            return carry

        lax.fori_loop(0, CX, keep_memory, 0)

    @pl.when(edge_y)
    def _():
        keep = keep_of_columns(widths_ref, start_y)[None]

        def layer(i, carry):
            flux = first_y(memory_y_in, i, 0)
            bend = second_y(i) + flux
            zeta = keep * zeta_y_in[i] + (keep - 1.0) * bend
            zeta_y[i] = zeta
            inside = slice(LO, LO + CY)
            following[i + H, :, inside, :] = following[i + H, :, inside, :] + speed[i] * (flux + zeta)
            grad = first_y(current, i, H)
            memory_y[i, :, inside, :] = keep * memory_y_in[i, :, inside, :] + (keep - 1.0) * grad
            return carry

        lax.fori_loop(0, CX, layer, 0)

    lane = lax.broadcasted_iota(jnp.int32, (1, LANES), 1)
    for s in range(NSRC):
        lx, ly, z = (sx[s] - start_x, sy[s] - start_y, sz[s])

        @pl.when((lx >= 0) & (lx < CX) & (ly >= 0) & (ly < CY))
        def _():
            at = (lx + H, z >> 7, pl.ds(ly + LO, 1), slice(None))
            added = jnp.where(lane == (z & 127), amp[step, s], 0.0)
            following[at] = following[at] + added

    if step > 0:
        observe(current, seen, step - 1, widths_ref, rx, ry, rz)


def join_kernel(last, *refs):
    if last:
        widths_ref, rx, ry, rz, speed, lo_x, hi_x, lo_y, hi_y, _, _, field, seen, beside = refs
    else:
        speed, lo_x, hi_x, lo_y, hi_y, _, field, up_x, down_x, up_y, down_y, beside = refs
    gx, gy, _, _ = place()
    has = [
        (gx > 0).astype(jnp.float32),
        (gx < lax.axis_size(GX) - 1).astype(jnp.float32),
        (gy > 0).astype(jnp.float32),
        (gy < lax.axis_size(GY) - 1).astype(jnp.float32),
    ]
    low_x, high_x, low_y, high_y = [[e * m for e in second_coef] for m in has]
    beside[:, :, 4:8, :] = lo_y[...]
    beside[:, :, 8:16, :] = jnp.zeros((CX, 2, 8, LANES), jnp.float32)
    beside[:, :, 16:20, :] = hi_y[...]

    def ends(i):
        first, final = (0.0, 0.0)
        for k in range(1, 5):
            first = first + low_y[k - 1] * beside[i, :, 8 - k : 16 - k, :]
            final = final + high_y[k - 1] * beside[i, :, 8 + k : 16 + k, :]
        return first, final

    def inside(i, carry):
        first, final = ends(i)
        for at, extra in ((0, first), (16, final)):
            rows = slice(LO + at, LO + at + 8)
            field[i + H, :, rows, :] = (
                field[i + H, :, rows, :] + speed[i, :, at : at + 8, :] * extra
            )
        return carry

    lax.fori_loop(H, CX - H, inside, 0, unroll=4)
    for r in range(H):
        for i, coef, halo in ((r, low_x, lo_x), (CX - H + r, high_x, hi_x)):
            across = 0.0
            for k in range(1, 5):
                at = H + i - k if i < H else i + k - CX
                if 0 <= at < H:
                    across = across + coef[k - 1] * halo[at]
            first, final = ends(i)
            for at, extra in ((0, first), (8, None), (16, final)):
                rows = slice(LO + at, LO + at + 8)
                part = across[:, at : at + 8, :]
                part = part if extra is None else part + extra
                field[i + H, :, rows, :] = (
                    field[i + H, :, rows, :] + speed[i, :, at : at + 8, :] * part
                )
    if last:
        observe(field, seen, STEPS - 1, widths_ref, rx, ry, rz)
    else:
        up_x[...] = field[CX : CX + H, :, LO : LO + CY, :]
        down_x[...] = field[H : 2 * H, :, LO : LO + CY, :]
        up_y[...] = field[H : H + CX, :, LO + CY - H : LO + CY, :]
        down_y[...] = field[H : H + CX, :, LO : LO + H, :]


def finish_kernel(field, pressure):
    for half in range(2):
        part = field[H : H + CX, half, LO : LO + CY, :]
        pressure[:, :, half * LANES : (half + 1) * LANES] = part


def vmem(count):
    return [pl.BlockSpec(memory_space=pltpu.VMEM)] * count


def smem(count):
    return [pl.BlockSpec(memory_space=pltpu.SMEM)] * count


def shape(*sizes):
    return [jax.ShapeDtypeStruct(size, jnp.float32) for size in sizes]


def ring(strip, axis, by):
    size = lax.axis_size(axis)
    return lax.ppermute(strip, axis, [(i, (i + by) % size) for i in range(size)])


def exchange(strips):
    up_x, down_x, up_y, down_y = strips
    return (ring(up_x, GX, 1), ring(down_x, GX, -1), ring(up_y, GY, 1), ring(down_y, GY, -1))


def spread(value, move):
    columns = lax.axis_size(GY)
    pairs = []
    for gx in range(lax.axis_size(GX)):
        for gy in range(columns):
            to_x, to_y = move(gx, gy)
            pairs.append((gx * columns + gy, to_x * columns + to_y))
    return lax.ppermute(value, BOTH, pairs)


def move_x(by, gx, gy):
    x = ((gy // 2) % 2) * 2 + gx % 2
    x = (x + by) % 4
    return (gx // 2) * 2 + x % 2, (gy // 4) * 4 + (x // 2) * 2 + gy % 2


def total(value):
    if (lax.axis_size(GX), lax.axis_size(GY)) != (8, 16):
        return lax.psum(value, BOTH)
    value = value + spread(value, lambda gx, gy: (gx, gy ^ 1))
    parts = [spread(value, functools.partial(move_x, by)) for by in (1, 2, 3)]
    value = value + parts[0] + parts[1] + parts[2]
    parts = [spread(value, lambda gx, gy, by=by: (gx, (gy + 4 * by) % 16)) for by in (1, 2, 3)]
    value = value + parts[0] + parts[1] + parts[2]
    parts = [spread(value, lambda gx, gy, by=by: ((gx + 2 * by) % 8, gy)) for by in (1, 2, 3)]
    return value + parts[0] + parts[1] + parts[2]


def per_device(
    pressure,
    pressure_old,
    speed_term,
    layer_width,
    source_x,
    source_y,
    source_z,
    source_amp,
    receiver_x,
    receiver_y,
    receiver_z,
):
    receivers = (receiver_x, receiver_y, receiver_z)
    limit = pltpu.CompilerParams(vmem_limit_bytes=48 * 1024 * 1024)
    strips_out = shape(STRIP_X, STRIP_X, STRIP_Y, STRIP_Y)
    current, *strips = pl.pallas_call(
        pack_kernel,
        out_shape=shape(FIELD) + strips_out,
        in_specs=vmem(1),
        out_specs=vmem(5),
        compiler_params=limit,
    )(pressure)
    previous, speed, *state = pl.pallas_call(
        begin_kernel,
        out_shape=shape(FIELD, BLOCK, MEM_X, MEM_Y, BLOCK, BLOCK, SEEN),
        in_specs=vmem(2),
        out_specs=vmem(7),
        compiler_params=limit,
    )(pressure_old, speed_term)
    band = jnp.asarray(band_matrix())
    for step in range(STEPS):
        halos = exchange(strips)
        following, *state = pl.pallas_call(
            functools.partial(inner_kernel, step),
            out_shape=shape(FIELD, MEM_X, MEM_Y, BLOCK, BLOCK, SEEN),
            in_specs=smem(8) + vmem(9),
            out_specs=vmem(6),
            scratch_shapes=[pltpu.VMEM(BLOCK, jnp.float32)],
            input_output_aliases={11: 0, 12: 1, 13: 2, 14: 3, 15: 4, 16: 5},
            compiler_params=limit,
        )(
            layer_width,
            source_x,
            source_y,
            source_z,
            source_amp,
            *receivers,
            band,
            current,
            speed,
            previous,
            *state,
        )
        previous = current
        beside = pltpu.VMEM((CX, 2, 24, LANES), jnp.float32)
        if step < STEPS - 1:
            current, *strips = pl.pallas_call(
                functools.partial(join_kernel, False),
                out_shape=shape(FIELD) + strips_out,
                in_specs=vmem(6),
                out_specs=vmem(5),
                scratch_shapes=[beside],
                input_output_aliases={5: 0},
                compiler_params=limit,
            )(speed, *halos, following)
        else:
            current, seen = pl.pallas_call(
                functools.partial(join_kernel, True),
                out_shape=shape(FIELD, SEEN),
                in_specs=smem(4) + vmem(7),
                out_specs=vmem(2),
                scratch_shapes=[beside],
                input_output_aliases={9: 0, 10: 1},
                compiler_params=limit,
            )(layer_width, *receivers, speed, *halos, following, state[-1])
    final = pl.pallas_call(
        finish_kernel,
        out_shape=jax.ShapeDtypeStruct(pressure.shape, jnp.float32),
        in_specs=vmem(1),
        out_specs=pl.BlockSpec(memory_space=pltpu.VMEM),
        compiler_params=limit,
    )(current)
    seen = total(seen)
    return final, seen[:STEPS, :NREC].T, jnp.sum(seen[STEPS:], axis=1)


def solution(mesh):
    block = P(GX, GY, None)
    return jax.shard_map(
        per_device,
        mesh=mesh,
        in_specs=(block, block, block) + (P(),) * 8,
        out_specs=(block, P(), P()),
        check_vma=False,
    )
```

```python
import functools

import jax
import jax.numpy as jnp
import ml_dtypes
import numpy as np
from jax import lax
from jax.experimental import pallas as pl
from jax.experimental.pallas import tpu as pltpu
from jax.sharding import PartitionSpec as P

STEPS = 8
NSRC = 4
NREC = 64
NX = 192
NY = 384
NZ = 256
CX = 24
CY = 24
H = 4
LO = 8
LANES = 128
GX = "gx"
GY = "gy"
BOTH = (GX, GY)

first_coef = (0.8, -0.2, 4.0 / 105.0, -1.0 / 280.0)
second_coef = (1.6, -0.2, 8.0 / 315.0, -1.0 / 560.0)
centre_coef = -205.0 / 72.0
damping = 0.6

FIELD = (CX + 2 * H, 2, CY + 2 * LO, LANES)
MEM_X = (2, CX + 2 * H, 2, CY, LANES)
MEM_Y = (CX, 2, CY + 2 * LO, LANES)
BLOCK = (CX, 2, CY, LANES)
STRIP_X = (H, 2, CY, LANES)
STRIP_Y = (CX, 2, H, LANES)
SEEN = (2 * STEPS, LANES)
KEEP_X = (CX, CY, LANES)
KEEP_Y = (CY, LANES)
NORM = (1, LANES)
RECEIVERS = 8
TABLE = RECEIVERS + NREC
COMMON = 5040.0
CHUNKS = 4
INSIDE = slice(LO, LO + CY)


def band_matrix():
    band = np.zeros((NZ, NZ), np.float32)
    for k, tap in enumerate((8064.0, -1008.0, 128.0, -9.0)):
        band += tap * (np.eye(NZ, k=k + 1) + np.eye(NZ, k=-k - 1)).astype(np.float32)
    return np.concatenate([band, band], axis=0).astype(ml_dtypes.bfloat16)


def profile(position, low_width, high_width, length):
    inward_low = jnp.clip((low_width - position) / low_width, 0.0, 1.0)
    inward_high = jnp.clip((position - (length - 1 - high_width)) / high_width, 0.0, 1.0)
    return jnp.exp(-damping * (inward_low * inward_low + inward_high * inward_high))


def wide(value):
    return jnp.full((1, LANES), value, jnp.float32)


def keep_of(widths, start, dims, dim, length):
    position = start + lax.broadcasted_iota(jnp.int32, dims, dim)
    low, high = [jnp.full(dims, w, jnp.float32) for w in widths]
    return profile(position.astype(jnp.float32), low, high, length)


def whole_sum(widths, length):
    rows = -(-length // LANES)
    index = lax.broadcasted_iota(jnp.int32, (rows, LANES), 0) * LANES
    index = index + lax.broadcasted_iota(jnp.int32, (rows, LANES), 1)
    value = profile(index.astype(jnp.float32), wide(widths[0]), wide(widths[1]), length)
    return jnp.sum(jnp.where(index < length, value, 0.0))


def place():
    gx, gy = (lax.axis_index(GX), lax.axis_index(GY))
    edge_x = (gx == 0) | (gx == lax.axis_size(GX) - 1)
    edge_y = (gy == 0) | (gy == lax.axis_size(GY) - 1)
    return gx, gy, edge_x, edge_y


def energy_row(field, i, keep_x, keep_y):
    weight = 1.0 - keep_x[i] * keep_y[...]
    value = field[i + H, :, INSIDE, :]
    return weight * (value[0] * value[0] + value[1] * value[1])


def note_energy(seen, step, summed, norm):
    at = STEPS + step
    seen[at : at + 1, :] = jnp.sum(summed, axis=0, keepdims=True) / norm[...]


def note_traces(field, seen, step, table):
    lane = lax.broadcasted_iota(jnp.int32, (1, LANES), 1)

    def sample(n, carry):
        code = table[RECEIVERS + n]
        r, z, ly, lx = (code & 63, (code >> 6) & 255, (code >> 14) & 31, code >> 19)
        line = field[lx + H, z >> 7, pl.ds(ly + LO, 1), :]
        turned = pltpu.roll(line, (r - (z & 127)) & 127, axis=1)
        seen[step : step + 1, :] = jnp.where(lane == r, turned, seen[step : step + 1, :])
        return carry

    lax.fori_loop(0, table[0], sample, 0)


def fetch(pairs, sems):
    copies = []
    for n, (source, target) in enumerate(pairs):
        for c in range(CHUNKS):
            rows = pl.ds(c * (CX // CHUNKS), CX // CHUNKS)
            copies.append(pltpu.make_async_copy(source.at[rows], target.at[rows], sems.at[n, c]))
    for copy in copies:
        copy.start()
    return copies


def split_strips(field, mine_x, mine_y, near_x, far_x, near_y, far_y):
    rows = [field[CX : CX + H, :, INSIDE, :], field[H : 2 * H, :, INSIDE, :]]
    near_x[...] = jnp.where(mine_x, rows[1], rows[0])
    far_x[...] = jnp.where(mine_x, rows[0], rows[1])
    high, low = (LO + CY - H, LO)
    columns = [field[H : H + CX, :, at : at + H, :] for at in (high, low)]
    near_y[...] = jnp.where(mine_y, columns[1], columns[0])
    far_y[...] = jnp.where(mine_y, columns[0], columns[1])


def odd():
    return lax.axis_index(GX) % 2 == 1, lax.axis_index(GY) % 2 == 1


def pack_kernel(pressure, field, near_x, far_x, near_y, far_y, staged, sems):
    copies = fetch([(pressure, staged)], sems)
    field[...] = jnp.zeros(FIELD, jnp.float32)
    for copy in copies:
        copy.wait()
    for half in range(2):
        part = staged[:, :, half * LANES : (half + 1) * LANES]
        field[H : H + CX, half, INSIDE, :] = part
    split_strips(field, *odd(), near_x, far_x, near_y, far_y)


def begin_kernel(
    widths_ref, sx, sy, sz, rx, ry, rz, old, speed_term,
    field, speed, memory_x, memory_y, zeta_x, zeta_y, seen, keep_x, keep_y, norm, table,
    staged_old, staged_speed, sems,
):
    copies = fetch([(old, staged_old), (speed_term, staged_speed)], sems)
    gx, gy, edge_x, edge_y = place()
    start_x, start_y = (gx * CX, gy * CY)
    seen[...] = jnp.zeros(SEEN, jnp.float32)
    field[...] = jnp.zeros(FIELD, jnp.float32)

    @pl.when(edge_x)
    def _():
        memory_x[...] = jnp.zeros(MEM_X, jnp.float32)
        zeta_x[...] = jnp.zeros(BLOCK, jnp.float32)

    @pl.when(edge_y)
    def _():
        memory_y[...] = jnp.zeros(MEM_Y, jnp.float32)
        zeta_y[...] = jnp.zeros(BLOCK, jnp.float32)

    @pl.when(edge_x | edge_y)
    def _():
        widths = [widths_ref[n].astype(jnp.float32) for n in range(4)]
        keep_x[...] = keep_of(widths[:2], start_x, KEEP_X, 0, NX)
        keep_y[...] = keep_of(widths[2:], start_y, KEEP_Y, 0, NY)
        cells = float(NX * NY) - whole_sum(widths[:2], NX) * whole_sum(widths[2:], NY)
        norm[...] = wide(float(NZ) * cells)

    def owned(px, py):
        lx, ly = (px - start_x, py - start_y)
        return lx, ly, (lx >= 0) & (lx < CX) & (ly >= 0) & (ly < CY)

    def add_receiver(r, count):
        lx, ly, here = owned(rx[r], ry[r])

        @pl.when(here)
        def _():
            table[RECEIVERS + count] = (((lx << 5) + ly) << 14) + (rz[r] << 6) + r

        return count + here.astype(jnp.int32)

    table[0] = lax.fori_loop(0, NREC, add_receiver, 0)

    def add_source(s, count):
        lx, ly, here = owned(sx[s], sy[s])

        @pl.when(here)
        def _():
            table[4 + count] = (((lx << 5) + ly) << 14) + (sz[s] << 6) + s

        return count + here.astype(jnp.int32)

    table[1] = lax.fori_loop(0, NSRC, add_source, 0)
    for copy in copies:
        copy.wait()
    for half in range(2):
        lanes = slice(half * LANES, (half + 1) * LANES)
        field[H : H + CX, half, INSIDE, :] = staged_old[:, :, lanes]
        speed[:, half, :, :] = staged_speed[:, :, lanes]


def inner_kernel(
    step, table, amp, band, current, speed, keep_x, keep_y, norm,
    previous, memory_x_in, memory_y_in, zeta_x_in, zeta_y_in, seen_in,
    following, memory_x, memory_y, zeta_x, zeta_y, seen, bend_z,
):
    _, _, edge_x, edge_y = place()
    halves = [current[H : H + CX, h, INSIDE, :].reshape(CX * CY, LANES) for h in range(2)]
    whole = jnp.concatenate(halves, axis=1)
    high = whole.astype(jnp.bfloat16)
    low = (whole - high.astype(jnp.float32)).astype(jnp.bfloat16)
    bent = jnp.dot(
        jnp.concatenate([high, low], axis=1), band[...], preferred_element_type=jnp.float32
    )
    for h in range(2):
        bend_z[:, h, :, :] = bent[:, h * LANES : (h + 1) * LANES].reshape(CX, CY, LANES)
    source, target = (step % 2, 1 - step % 2)

    def shifted_x(ref, lead, i, inside, k):
        return ref[lead + (i + k, slice(None), inside)]

    def sum_x(ref, lead, i, inside, sign, coef):
        total = 0.0
        for k in range(1, 5):
            up, down = (shifted_x(ref, lead, i, inside, k), shifted_x(ref, lead, i, inside, -k))
            total = total + coef[k - 1] * (up + down if sign > 0 else up - down)
        return total

    def sum_y(ref, i, sign, coef):
        total = 0.0
        for k in range(1, 5):
            up, down = (ref[i, :, LO + k : LO + CY + k, :], ref[i, :, LO - k : LO + CY - k, :])
            total = total + coef[k - 1] * (up + down if sign > 0 else up - down)
        return total

    def row(in_x, in_y, i, energy):
        centre = current[i + H, :, INSIDE, :]
        second_x = sum_x(current, (), i + H, INSIDE, 1, second_coef)
        second_y = sum_y(current, i + H, 1, second_coef)
        laplace = second_x + second_y + (3.0 * centre_coef) * centre + bend_z[i] * (1.0 / COMMON)
        every = slice(0, CY)
        if in_x:
            keep = keep_x[i]
            take = keep - 1.0
            flux = sum_x(memory_x_in, (source,), i + H, every, -1, first_coef)
            bend = second_x + centre_coef * centre + flux
            zeta = keep * zeta_x_in[i] + take * bend
            zeta_x[i] = zeta
            laplace = laplace + (flux + zeta)
            grad = sum_x(current, (), i + H, INSIDE, -1, first_coef)
            memory_x[target, i + H] = keep * memory_x_in[source, i + H] + take * grad
        if in_y:
            keep = keep_y[...]
            take = keep - 1.0
            flux = sum_y(memory_y_in, i, -1, first_coef)
            bend = second_y + centre_coef * centre + flux
            zeta = keep * zeta_y_in[i] + take * bend
            zeta_y[i] = zeta
            laplace = laplace + (flux + zeta)
            grad = sum_y(current, i + H, -1, first_coef)
            memory_y[i, :, INSIDE, :] = keep * memory_y_in[i, :, INSIDE, :] + take * grad
        value = 2.0 * centre - previous[i + H, :, INSIDE, :]
        following[i + H, :, INSIDE, :] = value + speed[i] * laplace
        if step > 0 and (in_x or in_y):
            energy = energy + energy_row(current, i, keep_x, keep_y)
        return energy

    for in_x in (False, True):
        for in_y in (False, True):

            @pl.when((edge_x == in_x) & (edge_y == in_y))
            def _():
                zero = jnp.zeros((CY, LANES), jnp.float32) if in_x or in_y else 0
                body = functools.partial(row, in_x, in_y)
                energy = lax.fori_loop(0, CX, body, zero, unroll=1 if in_x or in_y else 2)
                if step > 0 and (in_x or in_y):
                    note_energy(seen, step - 1, energy, norm)

    lane = lax.broadcasted_iota(jnp.int32, (1, LANES), 1)

    def inject(n, carry):
        code = table[4 + n]
        s, z, ly, lx = (code & 63, (code >> 6) & 255, (code >> 14) & 31, code >> 19)
        at = (lx + H, z >> 7, pl.ds(ly + LO, 1), slice(None))
        following[at] = following[at] + jnp.where(lane == (z & 127), amp[step, s], 0.0)
        return carry

    lax.fori_loop(0, table[1], inject, 0)
    if step > 0:
        note_traces(current, seen, step - 1, table)


def join_kernel(last, *refs):
    if last:
        table, keep_x, keep_y, norm, speed, near_x, far_x, near_y, far_y, _, _ = refs[:11]
        field, seen, beside = refs[11:]
    else:
        speed, near_x, far_x, near_y, far_y, _, field = refs[:7]
        strips, beside = (refs[7:11], refs[11])
    gx, gy, edge_x, edge_y = place()
    mine_x, mine_y = odd()
    halo_x = [jnp.where(mine_x, near_x[...], far_x[...]), jnp.where(mine_x, far_x[...], near_x[...])]
    has = [
        (gx > 0).astype(jnp.float32),
        (gx < lax.axis_size(GX) - 1).astype(jnp.float32),
        (gy > 0).astype(jnp.float32),
        (gy < lax.axis_size(GY) - 1).astype(jnp.float32),
    ]
    low_x, high_x, low_y, high_y = [[e * m for e in second_coef] for m in has]
    beside[:, :, 4:8, :] = jnp.where(mine_y, near_y[...], far_y[...])
    beside[:, :, 8:16, :] = jnp.zeros((CX, 2, 8, LANES), jnp.float32)
    beside[:, :, 16:20, :] = jnp.where(mine_y, far_y[...], near_y[...])

    def ends(i):
        first, final = (0.0, 0.0)
        for k in range(1, 5):
            first = first + low_y[k - 1] * beside[i, :, 8 - k : 16 - k, :]
            final = final + high_y[k - 1] * beside[i, :, 8 + k : 16 + k, :]
        return first, final

    def inside(i, carry):
        first, final = ends(i)
        for at, extra in ((0, first), (16, final)):
            rows = slice(LO + at, LO + at + 8)
            field[i + H, :, rows, :] = (
                field[i + H, :, rows, :] + speed[i, :, at : at + 8, :] * extra
            )
        return carry

    lax.fori_loop(H, CX - H, inside, 0, unroll=4)
    for r in range(H):
        for i, coef, halo in ((r, low_x, halo_x[0]), (CX - H + r, high_x, halo_x[1])):
            across = 0.0
            for k in range(1, 5):
                at = H + i - k if i < H else i + k - CX
                if 0 <= at < H:
                    across = across + coef[k - 1] * halo[at]
            first, final = ends(i)
            for at, extra in ((0, first), (8, None), (16, final)):
                rows = slice(LO + at, LO + at + 8)
                part = across[:, at : at + 8, :]
                part = part if extra is None else part + extra
                field[i + H, :, rows, :] = (
                    field[i + H, :, rows, :] + speed[i, :, at : at + 8, :] * part
                )
    if not last:
        split_strips(field, mine_x, mine_y, *strips)
        return

    @pl.when(edge_x | edge_y)
    def _():
        add = lambda i, summed: summed + energy_row(field, i, keep_x, keep_y)
        zero = jnp.zeros((CY, LANES), jnp.float32)
        note_energy(seen, STEPS - 1, lax.fori_loop(0, CX, add, zero, unroll=4), norm)

    note_traces(field, seen, STEPS - 1, table)


def finish_kernel(field, pressure):
    for half in range(2):
        part = field[H : H + CX, half, INSIDE, :]
        pressure[:, :, half * LANES : (half + 1) * LANES] = part


def report_kernel(*refs):
    parts, (traces, energy) = (refs[:-2], refs[-2:])
    seen = parts[0][...]
    for part in parts[1:]:
        seen = seen + part[...]
    turned = seen.T
    traces[...] = turned[:NREC, :STEPS]
    energy[...] = jnp.sum(turned[:, STEPS:], axis=0, keepdims=True)


def vmem(count):
    return [pl.BlockSpec(memory_space=pltpu.VMEM)] * count


def smem(count):
    return [pl.BlockSpec(memory_space=pltpu.SMEM)] * count


def hbm(count):
    return [pl.BlockSpec(memory_space=pl.ANY)] * count


def shape(*sizes):
    return [jax.ShapeDtypeStruct(size, jnp.float32) for size in sizes]


def limit(mebibytes):
    return pltpu.CompilerParams(vmem_limit_bytes=mebibytes * 1024 * 1024)


def swap(strip, axis, far):
    size = lax.axis_size(axis)
    return lax.ppermute(strip, axis, [(i, (((i + far) ^ 1) - far) % size) for i in range(size)])


def exchange(strips):
    near_x, far_x, near_y, far_y = strips
    return (swap(near_x, GX, 0), swap(far_x, GX, 1), swap(near_y, GY, 0), swap(far_y, GY, 1))


def spread(value, by):
    columns = lax.axis_size(GY)
    pairs = []
    for gx in range(lax.axis_size(GX)):
        for gy in range(columns):
            pairs.append((gx * columns + gy, (gx ^ by[0]) * columns + (gy ^ by[1])))
    return lax.ppermute(value, BOTH, pairs)


def gather_sums(value):
    if (lax.axis_size(GX), lax.axis_size(GY)) != (8, 16):
        return [lax.psum(value, BOTH)]
    parts = [value, spread(value, (0, 1))]
    for flips in (((1, 0), (0, 2), (1, 2)), ((0, 4), (0, 8), (0, 12)), ((2, 0), (4, 0), (6, 0))):
        value = functools.reduce(jnp.add, parts)
        parts = [value] + [spread(value, by) for by in flips]
    return parts


def per_device(
    pressure,
    pressure_old,
    speed_term,
    layer_width,
    source_x,
    source_y,
    source_z,
    source_amp,
    receiver_x,
    receiver_y,
    receiver_z,
):
    staged = pltpu.VMEM(pressure.shape, jnp.float32)
    strips_out = shape(STRIP_X, STRIP_X, STRIP_Y, STRIP_Y)
    current, *strips = pl.pallas_call(
        pack_kernel,
        out_shape=shape(FIELD) + strips_out,
        in_specs=hbm(1),
        out_specs=vmem(5),
        scratch_shapes=[staged, pltpu.SemaphoreType.DMA((1, CHUNKS))],
        compiler_params=limit(8),
    )(pressure)
    previous, speed, *rest = pl.pallas_call(
        begin_kernel,
        out_shape=shape(FIELD, BLOCK, MEM_X, MEM_Y, BLOCK, BLOCK, SEEN, KEEP_X, KEEP_Y, NORM)
        + [jax.ShapeDtypeStruct((TABLE,), jnp.int32)],
        in_specs=smem(7) + hbm(2),
        out_specs=vmem(10) + smem(1),
        scratch_shapes=[staged, staged, pltpu.SemaphoreType.DMA((2, CHUNKS))],
        compiler_params=limit(8),
    )(
        layer_width,
        source_x,
        source_y,
        source_z,
        receiver_x,
        receiver_y,
        receiver_z,
        pressure_old,
        speed_term,
    )
    state, keeps, table = (rest[:5], rest[5:8], rest[8])
    band = jnp.asarray(band_matrix())
    beside = pltpu.VMEM((CX, 2, 24, LANES), jnp.float32)
    for step in range(STEPS):
        halos = exchange(strips)
        following, *state = pl.pallas_call(
            functools.partial(inner_kernel, step),
            out_shape=shape(FIELD, MEM_X, MEM_Y, BLOCK, BLOCK, SEEN),
            in_specs=smem(2) + vmem(12),
            out_specs=vmem(6),
            scratch_shapes=[pltpu.VMEM(BLOCK, jnp.float32)],
            input_output_aliases={8: 0, 9: 1, 10: 2, 11: 3, 12: 4, 13: 5},
            compiler_params=limit(8),
        )(table, source_amp, band, current, speed, *keeps, previous, *state)
        previous = current
        if step < STEPS - 1:
            current, *strips = pl.pallas_call(
                functools.partial(join_kernel, False),
                out_shape=shape(FIELD) + strips_out,
                in_specs=vmem(6),
                out_specs=vmem(5),
                scratch_shapes=[beside],
                input_output_aliases={5: 0},
                compiler_params=limit(4),
            )(speed, *halos, following)
        else:
            current, seen = pl.pallas_call(
                functools.partial(join_kernel, True),
                out_shape=shape(FIELD, SEEN),
                in_specs=smem(1) + vmem(10),
                out_specs=vmem(2),
                scratch_shapes=[beside],
                input_output_aliases={9: 0, 10: 1},
                compiler_params=limit(4),
            )(table, *keeps, speed, *halos, following, state[-1])
    final = pl.pallas_call(
        finish_kernel,
        out_shape=jax.ShapeDtypeStruct(pressure.shape, jnp.float32),
        in_specs=vmem(1),
        out_specs=pl.BlockSpec(memory_space=pltpu.VMEM),
        compiler_params=limit(4),
    )(current)
    parts = gather_sums(seen)
    traces, energy = pl.pallas_call(
        report_kernel,
        out_shape=shape((NREC, STEPS), (1, STEPS)),
        in_specs=vmem(len(parts)),
        out_specs=vmem(2),
        compiler_params=limit(2),
    )(*parts)
    return final, traces, energy.reshape(STEPS)


def solution(mesh):
    block = P(GX, GY, None)
    return jax.shard_map(
        per_device,
        mesh=mesh,
        in_specs=(block, block, block) + (P(),) * 8,
        out_specs=(block, P(), P()),
        check_vma=False,
    )
```

```python
import functools

import jax
import jax.numpy as jnp
import ml_dtypes
import numpy as np
from jax import lax
from jax.experimental import pallas as pl
from jax.experimental.pallas import tpu as pltpu
from jax.sharding import PartitionSpec as P

STEPS = 8
NSRC = 4
NREC = 64
NX = 192
NY = 384
NZ = 256
CX = 24
CY = 24
H = 4
LO = 8
LANES = 128
GX = "gx"
GY = "gy"
BOTH = (GX, GY)

first_coef = (0.8, -0.2, 4.0 / 105.0, -1.0 / 280.0)
second_coef = (1.6, -0.2, 8.0 / 315.0, -1.0 / 560.0)
centre_coef = -205.0 / 72.0
damping = 0.6

FIELD = (CX + 2 * H, 2, CY + 2 * LO, LANES)
MEM_X = (2, CX + 2 * H, 2, CY, LANES)
MEM_Y = (CX, 2, CY + 2 * LO, LANES)
BLOCK = (CX, 2, CY, LANES)
STRIP_X = (H, 2, CY, LANES)
STRIP_Y = (CX, 2, H, LANES)
SEEN = (2 * STEPS, LANES)
KEEP_X = (CX, CY, LANES)
KEEP_Y = (CY, LANES)
NORM = (1, LANES)
RECEIVERS = 8
TABLE = RECEIVERS + NREC
COMMON = 5040.0
CHUNKS = 4
INSIDE = slice(LO, LO + CY)


def band_matrix():
    band = np.zeros((NZ, NZ), np.float32)
    for k, tap in enumerate((8064.0, -1008.0, 128.0, -9.0)):
        band += tap * (np.eye(NZ, k=k + 1) + np.eye(NZ, k=-k - 1)).astype(np.float32)
    return np.concatenate([band, band], axis=0).astype(ml_dtypes.bfloat16)


def profile(position, low_width, high_width, length):
    inward_low = jnp.clip((low_width - position) / low_width, 0.0, 1.0)
    inward_high = jnp.clip((position - (length - 1 - high_width)) / high_width, 0.0, 1.0)
    return jnp.exp(-damping * (inward_low * inward_low + inward_high * inward_high))


def wide(value):
    return jnp.full((1, LANES), value, jnp.float32)


def keep_of(widths, start, dims, dim, length):
    position = start + lax.broadcasted_iota(jnp.int32, dims, dim)
    low, high = [jnp.full(dims, w, jnp.float32) for w in widths]
    return profile(position.astype(jnp.float32), low, high, length)


def whole_sum(widths, length):
    rows = -(-length // LANES)
    index = lax.broadcasted_iota(jnp.int32, (rows, LANES), 0) * LANES
    index = index + lax.broadcasted_iota(jnp.int32, (rows, LANES), 1)
    value = profile(index.astype(jnp.float32), wide(widths[0]), wide(widths[1]), length)
    return jnp.sum(jnp.where(index < length, value, 0.0))


def place():
    gx, gy = (lax.axis_index(GX), lax.axis_index(GY))
    edge_x = (gx == 0) | (gx == lax.axis_size(GX) - 1)
    edge_y = (gy == 0) | (gy == lax.axis_size(GY) - 1)
    return gx, gy, edge_x, edge_y


def energy_row(field, i, keep_x, keep_y):
    weight = 1.0 - keep_x[i] * keep_y[...]
    value = field[i + H, :, INSIDE, :]
    return weight * (value[0] * value[0] + value[1] * value[1])


def note_energy(seen, step, summed, norm):
    at = STEPS + step
    seen[at : at + 1, :] = jnp.sum(summed, axis=0, keepdims=True) / norm[...]


def note_traces(field, seen, step, table):
    lane = lax.broadcasted_iota(jnp.int32, (1, LANES), 1)

    def sample(n, carry):
        code = table[RECEIVERS + n]
        r, z, ly, lx = (code & 63, (code >> 6) & 255, (code >> 14) & 31, code >> 19)
        line = field[lx + H, z >> 7, pl.ds(ly + LO, 1), :]
        turned = pltpu.roll(line, (r - (z & 127)) & 127, axis=1)
        seen[step : step + 1, :] = jnp.where(lane == r, turned, seen[step : step + 1, :])
        return carry

    lax.fori_loop(0, table[0], sample, 0)


def fetch(pairs, sems):
    copies = []
    for n, (source, target) in enumerate(pairs):
        for c in range(CHUNKS):
            rows = pl.ds(c * (CX // CHUNKS), CX // CHUNKS)
            copies.append(pltpu.make_async_copy(source.at[rows], target.at[rows], sems.at[n, c]))
    for copy in copies:
        copy.start()
    return copies


def split_strips(field, mine_x, mine_y, near_x, far_x, near_y, far_y):
    rows = [field[CX : CX + H, :, INSIDE, :], field[H : 2 * H, :, INSIDE, :]]
    near_x[...] = jnp.where(mine_x, rows[1], rows[0])
    far_x[...] = jnp.where(mine_x, rows[0], rows[1])
    high, low = (LO + CY - H, LO)
    columns = [field[H : H + CX, :, at : at + H, :] for at in (high, low)]
    near_y[...] = jnp.where(mine_y, columns[1], columns[0])
    far_y[...] = jnp.where(mine_y, columns[0], columns[1])


def odd():
    return lax.axis_index(GX) % 2 == 1, lax.axis_index(GY) % 2 == 1


def pack_kernel(pressure, field, near_x, far_x, near_y, far_y, staged, sems):
    copies = fetch([(pressure, staged)], sems)
    field[...] = jnp.zeros(FIELD, jnp.float32)
    for copy in copies:
        copy.wait()
    for half in range(2):
        part = staged[:, :, half * LANES : (half + 1) * LANES]
        field[H : H + CX, half, INSIDE, :] = part
    split_strips(field, *odd(), near_x, far_x, near_y, far_y)


def begin_kernel(
    widths_far, sx_far, sy_far, sz_far, rx_far, ry_far, rz_far, amp_far, old, speed_term,
    field, speed, memory_x, memory_y, zeta_x, zeta_y, seen, keep_x, keep_y, norm, table, amps,
    staged_old, staged_speed, sems, widths_ref, sx, sy, sz, rx, ry, rz, amp, small_sems,
):
    far = (widths_far, sx_far, sy_far, sz_far, rx_far, ry_far, rz_far, amp_far)
    near = (widths_ref, sx, sy, sz, rx, ry, rz, amp)
    small = [
        pltpu.make_async_copy(source, target, small_sems.at[n])
        for n, (source, target) in enumerate(zip(far, near))
    ]
    for copy in small:
        copy.start()
    copies = fetch([(old, staged_old), (speed_term, staged_speed)], sems)
    gx, gy, edge_x, edge_y = place()
    start_x, start_y = (gx * CX, gy * CY)
    seen[...] = jnp.zeros(SEEN, jnp.float32)
    field[...] = jnp.zeros(FIELD, jnp.float32)

    @pl.when(edge_x)
    def _():
        memory_x[...] = jnp.zeros(MEM_X, jnp.float32)
        zeta_x[...] = jnp.zeros(BLOCK, jnp.float32)

    @pl.when(edge_y)
    def _():
        memory_y[...] = jnp.zeros(MEM_Y, jnp.float32)
        zeta_y[...] = jnp.zeros(BLOCK, jnp.float32)

    for copy in small:
        copy.wait()

    @pl.when(edge_x | edge_y)
    def _():
        widths = [widths_ref[n].astype(jnp.float32) for n in range(4)]
        keep = keep_of(widths[:2], start_x, KEEP_Y, 0, NX)
        for i in range(CX):
            keep_x[i] = jnp.broadcast_to(keep[i : i + 1], KEEP_Y)
        keep_y[...] = keep_of(widths[2:], start_y, KEEP_Y, 0, NY)
        cells = float(NX * NY) - whole_sum(widths[:2], NX) * whole_sum(widths[2:], NY)
        norm[...] = wide(float(NZ) * cells)

    def owned(px, py):
        lx, ly = (px - start_x, py - start_y)
        return lx, ly, (lx >= 0) & (lx < CX) & (ly >= 0) & (ly < CY)

    def note(at, n, px, py, pz):
        def add(r, count):
            lx, ly, here = owned(px[r], py[r])

            @pl.when(here)
            def _():
                table[at + count] = (((lx << 5) + ly) << 14) + (pz[r] << 6) + r

            return count + here.astype(jnp.int32)

        return lax.fori_loop(0, n, add, 0)

    table[0] = note(RECEIVERS, NREC, rx, ry, rz)
    table[1] = note(4, NSRC, sx, sy, sz)
    for t in range(STEPS):
        for n in range(NSRC):
            amps[t * NSRC + n] = amp[t, n]
    for copy in copies:
        copy.wait()
    for half in range(2):
        lanes = slice(half * LANES, (half + 1) * LANES)
        field[H : H + CX, half, INSIDE, :] = staged_old[:, :, lanes]
        speed[:, half, :, :] = staged_speed[:, :, lanes]


def inner_kernel(
    step, table, amps, band, current, speed, keep_x, keep_y, norm,
    previous, memory_x_in, memory_y_in, zeta_x_in, zeta_y_in, seen_in,
    following, memory_x, memory_y, zeta_x, zeta_y, seen, bend_z,
):
    _, _, edge_x, edge_y = place()
    halves = [current[H : H + CX, h, INSIDE, :].reshape(CX * CY, LANES) for h in range(2)]
    whole = jnp.concatenate(halves, axis=1)
    high = whole.astype(jnp.bfloat16)
    low = (whole - high.astype(jnp.float32)).astype(jnp.bfloat16)
    bent = jnp.dot(
        jnp.concatenate([high, low], axis=1), band[...], preferred_element_type=jnp.float32
    )
    for h in range(2):
        bend_z[:, h, :, :] = bent[:, h * LANES : (h + 1) * LANES].reshape(CX, CY, LANES)
    source, target = (step % 2, 1 - step % 2)

    def taps(pick, want_first):
        second, first = (0.0, 0.0)
        for k in range(1, 5):
            up, down = (pick(k), pick(-k))
            second = second + second_coef[k - 1] * (up + down)
            if want_first:
                first = first + first_coef[k - 1] * (up - down)
        return second, first

    def first_only(pick):
        total = 0.0
        for k in range(1, 5):
            total = total + first_coef[k - 1] * (pick(k) - pick(-k))
        return total

    def row(in_x, in_y, damped, i, energy):
        for h in range(2):
            centre = current[i + H, h, INSIDE, :]
            second_x, grad_x = taps(lambda k: current[i + H + k, h, INSIDE, :], in_x)
            second_y, grad_y = taps(lambda k: current[i + H, h, LO + k : LO + CY + k, :], in_y)
            laplace = second_x + second_y + (3.0 * centre_coef) * centre
            laplace = laplace + bend_z[i, h] * (1.0 / COMMON)
            if in_x:
                keep = keep_x[i]
                take = keep - 1.0
                flux = first_only(lambda k: memory_x_in[source, i + H + k, h])
                bend = second_x + centre_coef * centre + flux
                zeta = keep * zeta_x_in[i, h] + take * bend
                zeta_x[i, h] = zeta
                laplace = laplace + (flux + zeta)
                memory_x[target, i + H, h] = keep * memory_x_in[source, i + H, h] + take * grad_x
            if in_y:
                keep = keep_y[...]
                take = keep - 1.0
                flux = first_only(lambda k: memory_y_in[i, h, LO + k : LO + CY + k, :])
                bend = second_y + centre_coef * centre + flux
                zeta = keep * zeta_y_in[i, h] + take * bend
                zeta_y[i, h] = zeta
                laplace = laplace + (flux + zeta)
                kept = keep * memory_y_in[i, h, INSIDE, :] + take * grad_y
                memory_y[i, h, INSIDE, :] = kept
            value = 2.0 * centre - previous[i + H, h, INSIDE, :]
            following[i + H, h, INSIDE, :] = value + speed[i, h] * laplace
            if step > 0 and damped:
                energy = energy + (1.0 - keep_x[i] * keep_y[...]) * (centre * centre)
        return energy

    for is_x in (False, True):
        for is_y in (False, True):

            @pl.when((edge_x == is_x) & (edge_y == is_y))
            def _():
                damped = is_x or is_y
                energy = jnp.zeros((CY, LANES), jnp.float32) if damped else 0
                body = functools.partial(row, is_x, is_y, damped)
                if is_x:
                    starts_low = lax.axis_index(GX) == 0
                    first = jnp.where(starts_low, 0, H)
                    energy = lax.fori_loop(first, first + CX - H, body, energy)
                    rest = jnp.where(starts_low, CX - H, 0)
                    body = functools.partial(row, False, is_y, damped)
                    energy = lax.fori_loop(rest, rest + H, body, energy)
                else:
                    energy = lax.fori_loop(0, CX, body, energy, unroll=2)
                if step > 0 and damped:
                    note_energy(seen, step - 1, energy, norm)

    lane = lax.broadcasted_iota(jnp.int32, (1, LANES), 1)

    def inject(n, carry):
        code = table[4 + n]
        s, z, ly, lx = (code & 63, (code >> 6) & 255, (code >> 14) & 31, code >> 19)
        at = (lx + H, z >> 7, pl.ds(ly + LO, 1), slice(None))
        following[at] = following[at] + jnp.where(lane == (z & 127), amps[step * NSRC + s], 0.0)
        return carry

    lax.fori_loop(0, table[1], inject, 0)
    if step > 0:
        note_traces(current, seen, step - 1, table)


def join_kernel(last, *refs):
    if last:
        table, keep_x, keep_y, norm, speed, near_x, far_x, near_y, far_y, _, _ = refs[:11]
        field, seen, beside = refs[11:]
    else:
        speed, near_x, far_x, near_y, far_y, _, field = refs[:7]
        strips, beside = (refs[7:11], refs[11])
    gx, gy, edge_x, edge_y = place()
    mine_x, mine_y = odd()
    halo_x = [jnp.where(mine_x, near_x[...], far_x[...]), jnp.where(mine_x, far_x[...], near_x[...])]
    has = [
        (gx > 0).astype(jnp.float32),
        (gx < lax.axis_size(GX) - 1).astype(jnp.float32),
        (gy > 0).astype(jnp.float32),
        (gy < lax.axis_size(GY) - 1).astype(jnp.float32),
    ]
    low_x, high_x, low_y, high_y = [[e * m for e in second_coef] for m in has]
    beside[:, :, 4:8, :] = jnp.where(mine_y, near_y[...], far_y[...])
    beside[:, :, 8:16, :] = jnp.zeros((CX, 2, 8, LANES), jnp.float32)
    beside[:, :, 16:20, :] = jnp.where(mine_y, far_y[...], near_y[...])

    def ends(i):
        first, final = (0.0, 0.0)
        for k in range(1, 5):
            first = first + low_y[k - 1] * beside[i, :, 8 - k : 16 - k, :]
            final = final + high_y[k - 1] * beside[i, :, 8 + k : 16 + k, :]
        return first, final

    def inside(i, carry):
        first, final = ends(i)
        for at, extra in ((0, first), (16, final)):
            rows = slice(LO + at, LO + at + 8)
            field[i + H, :, rows, :] = (
                field[i + H, :, rows, :] + speed[i, :, at : at + 8, :] * extra
            )
        return carry

    lax.fori_loop(H, CX - H, inside, 0, unroll=4)
    for r in range(H):
        for i, coef, halo in ((r, low_x, halo_x[0]), (CX - H + r, high_x, halo_x[1])):
            across = 0.0
            for k in range(1, 5):
                at = H + i - k if i < H else i + k - CX
                if 0 <= at < H:
                    across = across + coef[k - 1] * halo[at]
            first, final = ends(i)
            for at, extra in ((0, first), (8, None), (16, final)):
                rows = slice(LO + at, LO + at + 8)
                part = across[:, at : at + 8, :]
                part = part if extra is None else part + extra
                field[i + H, :, rows, :] = (
                    field[i + H, :, rows, :] + speed[i, :, at : at + 8, :] * part
                )
    if not last:
        split_strips(field, mine_x, mine_y, *strips)
        return

    @pl.when(edge_x | edge_y)
    def _():
        add = lambda i, summed: summed + energy_row(field, i, keep_x, keep_y)
        zero = jnp.zeros((CY, LANES), jnp.float32)
        note_energy(seen, STEPS - 1, lax.fori_loop(0, CX, add, zero, unroll=4), norm)

    note_traces(field, seen, STEPS - 1, table)


def finish_kernel(field, pressure):
    for half in range(2):
        part = field[H : H + CX, half, INSIDE, :]
        pressure[:, :, half * LANES : (half + 1) * LANES] = part


def report_kernel(*refs):
    parts, (traces, energy) = (refs[:-2], refs[-2:])
    seen = parts[0][...]
    for part in parts[1:]:
        seen = seen + part[...]
    turned = seen.T
    traces[...] = turned[:NREC, :STEPS]
    energy[...] = jnp.sum(turned[:, STEPS:], axis=0)


def vmem(count):
    return [pl.BlockSpec(memory_space=pltpu.VMEM)] * count


def smem(count):
    return [pl.BlockSpec(memory_space=pltpu.SMEM)] * count


def hbm(count):
    return [pl.BlockSpec(memory_space=pltpu.HBM)] * count


def shape(*sizes):
    return [jax.ShapeDtypeStruct(size, jnp.float32) for size in sizes]


def limit(mebibytes):
    return pltpu.CompilerParams(vmem_limit_bytes=mebibytes * 1024 * 1024)


def swap(strip, axis, far):
    size = lax.axis_size(axis)
    return lax.ppermute(strip, axis, [(i, (((i + far) ^ 1) - far) % size) for i in range(size)])


def exchange(strips):
    near_x, far_x, near_y, far_y = strips
    return (swap(near_x, GX, 0), swap(far_x, GX, 1), swap(near_y, GY, 0), swap(far_y, GY, 1))


def spread(value, by):
    columns = lax.axis_size(GY)
    pairs = []
    for gx in range(lax.axis_size(GX)):
        for gy in range(columns):
            pairs.append((gx * columns + gy, (gx ^ by[0]) * columns + (gy ^ by[1])))
    return lax.ppermute(value, BOTH, pairs)


def gather_sums(value):
    if (lax.axis_size(GX), lax.axis_size(GY)) != (8, 16):
        return [lax.psum(value, BOTH)]
    parts = [value, spread(value, (0, 1))]
    for flips in (((1, 0), (0, 2), (1, 2)), ((0, 4), (0, 8), (0, 12)), ((2, 0), (4, 0), (6, 0))):
        value = functools.reduce(jnp.add, parts)
        parts = [value] + [spread(value, by) for by in flips]
    return parts


def per_device(
    pressure,
    pressure_old,
    speed_term,
    layer_width,
    source_x,
    source_y,
    source_z,
    source_amp,
    receiver_x,
    receiver_y,
    receiver_z,
):
    staged = pltpu.VMEM(pressure.shape, jnp.float32)
    strips_out = shape(STRIP_X, STRIP_X, STRIP_Y, STRIP_Y)
    current, *strips = pl.pallas_call(
        pack_kernel,
        out_shape=shape(FIELD) + strips_out,
        in_specs=hbm(1),
        out_specs=vmem(5),
        scratch_shapes=[staged, pltpu.SemaphoreType.DMA((1, CHUNKS))],
        compiler_params=limit(8),
    )(pressure)
    previous, speed, *rest = pl.pallas_call(
        begin_kernel,
        out_shape=shape(FIELD, BLOCK, MEM_X, MEM_Y, BLOCK, BLOCK, SEEN, KEEP_X, KEEP_Y, NORM)
        + [
            jax.ShapeDtypeStruct((TABLE,), jnp.int32),
            jax.ShapeDtypeStruct((STEPS * NSRC,), jnp.float32),
        ],
        in_specs=hbm(10),
        out_specs=vmem(10) + smem(2),
        scratch_shapes=[staged, staged, pltpu.SemaphoreType.DMA((2, CHUNKS))]
        + [pltpu.SMEM((n,), jnp.int32) for n in (4, NSRC, NSRC, NSRC, NREC, NREC, NREC)]
        + [pltpu.SMEM((STEPS, NSRC), jnp.float32), pltpu.SemaphoreType.DMA((8,))],
        compiler_params=limit(8),
    )(
        layer_width,
        source_x,
        source_y,
        source_z,
        receiver_x,
        receiver_y,
        receiver_z,
        source_amp,
        pressure_old,
        speed_term,
    )
    state, keeps, table, amps = (rest[:5], rest[5:8], rest[8], rest[9])
    band = jnp.asarray(band_matrix())
    beside = pltpu.VMEM((CX, 2, 24, LANES), jnp.float32)
    for step in range(STEPS):
        halos = exchange(strips)
        following, *state = pl.pallas_call(
            functools.partial(inner_kernel, step),
            out_shape=shape(FIELD, MEM_X, MEM_Y, BLOCK, BLOCK, SEEN),
            in_specs=smem(2) + vmem(12),
            out_specs=vmem(6),
            scratch_shapes=[pltpu.VMEM(BLOCK, jnp.float32)],
            input_output_aliases={8: 0, 9: 1, 10: 2, 11: 3, 12: 4, 13: 5},
            compiler_params=limit(8),
        )(table, amps, band, current, speed, *keeps, previous, *state)
        previous = current
        if step < STEPS - 1:
            current, *strips = pl.pallas_call(
                functools.partial(join_kernel, False),
                out_shape=shape(FIELD) + strips_out,
                in_specs=vmem(6),
                out_specs=vmem(5),
                scratch_shapes=[beside],
                input_output_aliases={5: 0},
                compiler_params=limit(4),
            )(speed, *halos, following)
        else:
            current, seen = pl.pallas_call(
                functools.partial(join_kernel, True),
                out_shape=shape(FIELD, SEEN),
                in_specs=smem(1) + vmem(10),
                out_specs=vmem(2),
                scratch_shapes=[beside],
                input_output_aliases={9: 0, 10: 1},
                compiler_params=limit(4),
            )(table, *keeps, speed, *halos, following, state[-1])
    final = pl.pallas_call(
        finish_kernel,
        out_shape=jax.ShapeDtypeStruct(pressure.shape, jnp.float32),
        in_specs=vmem(1),
        out_specs=pl.BlockSpec(memory_space=pltpu.VMEM),
        compiler_params=limit(4),
    )(current)
    parts = gather_sums(seen)
    traces, energy = pl.pallas_call(
        report_kernel,
        out_shape=shape((NREC, STEPS), (STEPS,)),
        in_specs=vmem(len(parts)),
        out_specs=vmem(2),
        compiler_params=limit(2),
    )(*parts)
    return final, traces, energy


def solution(mesh):
    block = P(GX, GY, None)
    return jax.shard_map(
        per_device,
        mesh=mesh,
        in_specs=(block, block, block) + (P(),) * 8,
        out_specs=(block, P(), P()),
        check_vma=False,
    )
```

```python
import functools

import jax
import jax.numpy as jnp
import ml_dtypes
import numpy as np
from jax import lax
from jax.experimental import pallas as pl
from jax.experimental.pallas import tpu as pltpu
from jax.sharding import PartitionSpec as P

STEPS = 8
NSRC = 4
NREC = 64
NX = 192
NY = 384
NZ = 256
CX = 24
CY = 24
H = 4
LO = 8
LANES = 128
GX = "gx"
GY = "gy"
BOTH = (GX, GY)

first_coef = (0.8, -0.2, 4.0 / 105.0, -1.0 / 280.0)
second_coef = (1.6, -0.2, 8.0 / 315.0, -1.0 / 560.0)
centre_coef = -205.0 / 72.0
damping = 0.6

FIELD = (CX + 2 * H, 2, CY + 2 * LO, LANES)
MEM_X = (2, CX + 2 * H, 2, CY, LANES)
MEM_Y = (CX, 2, CY + 2 * LO, LANES)
BLOCK = (CX, 2, CY, LANES)
STRIP_X = (H, 2, CY, LANES)
STRIP_Y = (CX, 2, H, LANES)
SEEN = (2 * STEPS, LANES)
KEEP_X = (CX, CY, LANES)
KEEP_Y = (CY, LANES)
NORM = (1, LANES)
RECEIVERS = 8
TABLE = RECEIVERS + NREC
COMMON = 5040.0
CHUNKS = 4
INSIDE = slice(LO, LO + CY)


def band_matrix():
    band = np.zeros((NZ, NZ), np.float32)
    for k, tap in enumerate((8064.0, -1008.0, 128.0, -9.0)):
        band += tap * (np.eye(NZ, k=k + 1) + np.eye(NZ, k=-k - 1)).astype(np.float32)
    return np.concatenate([band, band], axis=0).astype(ml_dtypes.bfloat16)


def profile(position, low_width, high_width, length):
    inward_low = jnp.clip((low_width - position) / low_width, 0.0, 1.0)
    inward_high = jnp.clip((position - (length - 1 - high_width)) / high_width, 0.0, 1.0)
    return jnp.exp(-damping * (inward_low * inward_low + inward_high * inward_high))


def wide(value):
    return jnp.full((1, LANES), value, jnp.float32)


def keep_of(widths, start, dims, dim, length):
    position = start + lax.broadcasted_iota(jnp.int32, dims, dim)
    low, high = [jnp.full(dims, w, jnp.float32) for w in widths]
    return profile(position.astype(jnp.float32), low, high, length)


def whole_sum(widths, length):
    rows = -(-length // LANES)
    index = lax.broadcasted_iota(jnp.int32, (rows, LANES), 0) * LANES
    index = index + lax.broadcasted_iota(jnp.int32, (rows, LANES), 1)
    value = profile(index.astype(jnp.float32), wide(widths[0]), wide(widths[1]), length)
    return jnp.sum(jnp.where(index < length, value, 0.0))


def place():
    gx, gy = (lax.axis_index(GX), lax.axis_index(GY))
    edge_x = (gx == 0) | (gx == lax.axis_size(GX) - 1)
    edge_y = (gy == 0) | (gy == lax.axis_size(GY) - 1)
    return gx, gy, edge_x, edge_y


def energy_row(field, i, keep_x, keep_y):
    weight = 1.0 - keep_x[i] * keep_y[...]
    value = field[i + H, :, INSIDE, :]
    return weight * (value[0] * value[0] + value[1] * value[1])


def note_energy(seen, step, summed, norm):
    at = STEPS + step
    seen[at : at + 1, :] = jnp.sum(summed, axis=0, keepdims=True) / norm[...]


def note_traces(field, seen, step, table):
    lane = lax.broadcasted_iota(jnp.int32, (1, LANES), 1)

    def sample(n, carry):
        code = table[RECEIVERS + n]
        r, z, ly, lx = (code & 63, (code >> 6) & 255, (code >> 14) & 31, code >> 19)
        line = field[lx + H, z >> 7, pl.ds(ly + LO, 1), :]
        turned = pltpu.roll(line, (r - (z & 127)) & 127, axis=1)
        seen[step : step + 1, :] = jnp.where(lane == r, turned, seen[step : step + 1, :])
        return carry

    lax.fori_loop(0, table[0], sample, 0)


def fetch(pairs, sems):
    copies = []
    for n, (source, target) in enumerate(pairs):
        for c in range(CHUNKS):
            rows = pl.ds(c * (CX // CHUNKS), CX // CHUNKS)
            copies.append(pltpu.make_async_copy(source.at[rows], target.at[rows], sems.at[n, c]))
    for copy in copies:
        copy.start()
    return copies


def split_strips(field, mine_x, mine_y, near_x, far_x, near_y, far_y):
    rows = [field[CX : CX + H, :, INSIDE, :], field[H : 2 * H, :, INSIDE, :]]
    near_x[...] = jnp.where(mine_x, rows[1], rows[0])
    far_x[...] = jnp.where(mine_x, rows[0], rows[1])
    high, low = (LO + CY - H, LO)
    columns = [field[H : H + CX, :, at : at + H, :] for at in (high, low)]
    near_y[...] = jnp.where(mine_y, columns[1], columns[0])
    far_y[...] = jnp.where(mine_y, columns[0], columns[1])


def odd():
    return lax.axis_index(GX) % 2 == 1, lax.axis_index(GY) % 2 == 1


def pack_kernel(pressure, field, near_x, far_x, near_y, far_y, staged, sems):
    copies = fetch([(pressure, staged)], sems)
    field[...] = jnp.zeros(FIELD, jnp.float32)
    for copy in copies:
        copy.wait()
    for half in range(2):
        part = staged[:, :, half * LANES : (half + 1) * LANES]
        field[H : H + CX, half, INSIDE, :] = part
    split_strips(field, *odd(), near_x, far_x, near_y, far_y)


def begin_kernel(
    widths_far, sx_far, sy_far, sz_far, rx_far, ry_far, rz_far, amp_far, old, speed_term,
    field, speed, memory_x, memory_y, zeta_x, zeta_y, seen, keep_x, keep_y, norm, table, amps,
    staged_old, staged_speed, sems, widths_ref, sx, sy, sz, rx, ry, rz, amp, small_sems,
):
    far = (widths_far, sx_far, sy_far, sz_far, rx_far, ry_far, rz_far, amp_far)
    near = (widths_ref, sx, sy, sz, rx, ry, rz, amp)
    small = [
        pltpu.make_async_copy(source, target, small_sems.at[n])
        for n, (source, target) in enumerate(zip(far, near))
    ]
    for copy in small:
        copy.start()
    copies = fetch([(old, staged_old), (speed_term, staged_speed)], sems)
    gx, gy, edge_x, edge_y = place()
    start_x, start_y = (gx * CX, gy * CY)
    seen[...] = jnp.zeros(SEEN, jnp.float32)
    field[...] = jnp.zeros(FIELD, jnp.float32)

    @pl.when(edge_x)
    def _():
        memory_x[...] = jnp.zeros(MEM_X, jnp.float32)
        zeta_x[...] = jnp.zeros(BLOCK, jnp.float32)

    @pl.when(edge_y)
    def _():
        memory_y[...] = jnp.zeros(MEM_Y, jnp.float32)
        zeta_y[...] = jnp.zeros(BLOCK, jnp.float32)

    for copy in small:
        copy.wait()

    @pl.when(edge_x | edge_y)
    def _():
        widths = [widths_ref[n].astype(jnp.float32) for n in range(4)]
        keep = keep_of(widths[:2], start_x, KEEP_Y, 0, NX)
        for i in range(CX):
            keep_x[i] = jnp.broadcast_to(keep[i : i + 1], KEEP_Y)
        keep_y[...] = keep_of(widths[2:], start_y, KEEP_Y, 0, NY)
        cells = float(NX * NY) - whole_sum(widths[:2], NX) * whole_sum(widths[2:], NY)
        norm[...] = wide(float(NZ) * cells)

    def owned(px, py):
        lx, ly = (px - start_x, py - start_y)
        return lx, ly, (lx >= 0) & (lx < CX) & (ly >= 0) & (ly < CY)

    def note(at, n, px, py, pz):
        def add(r, count):
            lx, ly, here = owned(px[r], py[r])

            @pl.when(here)
            def _():
                table[at + count] = (((lx << 5) + ly) << 14) + (pz[r] << 6) + r

            return count + here.astype(jnp.int32)

        return lax.fori_loop(0, n, add, 0)

    table[0] = note(RECEIVERS, NREC, rx, ry, rz)
    table[1] = note(4, NSRC, sx, sy, sz)
    for t in range(STEPS):
        for n in range(NSRC):
            amps[t * NSRC + n] = amp[n, t]
    for copy in copies:
        copy.wait()
    for half in range(2):
        lanes = slice(half * LANES, (half + 1) * LANES)
        field[H : H + CX, half, INSIDE, :] = staged_old[:, :, lanes]
        speed[:, half, :, :] = staged_speed[:, :, lanes]


def inner_kernel(
    step, table, amps, band, current, speed, keep_x, keep_y, norm,
    previous, memory_x_in, memory_y_in, zeta_x_in, zeta_y_in, seen_in,
    following, memory_x, memory_y, zeta_x, zeta_y, seen, bend_z,
):
    _, _, edge_x, edge_y = place()
    halves = [current[H : H + CX, h, INSIDE, :].reshape(CX * CY, LANES) for h in range(2)]
    whole = jnp.concatenate(halves, axis=1)
    high = whole.astype(jnp.bfloat16)
    low = (whole - high.astype(jnp.float32)).astype(jnp.bfloat16)
    bent = jnp.dot(
        jnp.concatenate([high, low], axis=1), band[...], preferred_element_type=jnp.float32
    )
    for h in range(2):
        bend_z[:, h, :, :] = bent[:, h * LANES : (h + 1) * LANES].reshape(CX, CY, LANES)
    source, target = (step % 2, 1 - step % 2)

    def taps(pick, want_first):
        second, first = (0.0, 0.0)
        for k in range(1, 5):
            up, down = (pick(k), pick(-k))
            second = second + second_coef[k - 1] * (up + down)
            if want_first:
                first = first + first_coef[k - 1] * (up - down)
        return second, first

    def first_only(pick):
        total = 0.0
        for k in range(1, 5):
            total = total + first_coef[k - 1] * (pick(k) - pick(-k))
        return total

    def row(in_x, in_y, damped, i, energy):
        for h in range(2):
            centre = current[i + H, h, INSIDE, :]
            second_x, grad_x = taps(lambda k: current[i + H + k, h, INSIDE, :], in_x)
            second_y, grad_y = taps(lambda k: current[i + H, h, LO + k : LO + CY + k, :], in_y)
            laplace = second_x + second_y + (3.0 * centre_coef) * centre
            laplace = laplace + bend_z[i, h] * (1.0 / COMMON)
            if in_x:
                keep = keep_x[i]
                take = keep - 1.0
                flux = first_only(lambda k: memory_x_in[source, i + H + k, h])
                bend = second_x + centre_coef * centre + flux
                zeta = keep * zeta_x_in[i, h] + take * bend
                zeta_x[i, h] = zeta
                laplace = laplace + (flux + zeta)
                memory_x[target, i + H, h] = keep * memory_x_in[source, i + H, h] + take * grad_x
            if in_y:
                keep = keep_y[...]
                take = keep - 1.0
                flux = first_only(lambda k: memory_y_in[i, h, LO + k : LO + CY + k, :])
                bend = second_y + centre_coef * centre + flux
                zeta = keep * zeta_y_in[i, h] + take * bend
                zeta_y[i, h] = zeta
                laplace = laplace + (flux + zeta)
                kept = keep * memory_y_in[i, h, INSIDE, :] + take * grad_y
                memory_y[i, h, INSIDE, :] = kept
            value = 2.0 * centre - previous[i + H, h, INSIDE, :]
            following[i + H, h, INSIDE, :] = value + speed[i, h] * laplace
            if step > 0 and damped:
                energy = energy + (1.0 - keep_x[i] * keep_y[...]) * (centre * centre)
        return energy

    for is_x in (False, True):
        for is_y in (False, True):

            @pl.when((edge_x == is_x) & (edge_y == is_y))
            def _():
                damped = is_x or is_y
                energy = jnp.zeros((CY, LANES), jnp.float32) if damped else 0
                body = functools.partial(row, is_x, is_y, damped)
                if is_x:
                    starts_low = lax.axis_index(GX) == 0
                    first = jnp.where(starts_low, 0, H)
                    energy = lax.fori_loop(first, first + CX - H, body, energy)
                    rest = jnp.where(starts_low, CX - H, 0)
                    body = functools.partial(row, False, is_y, damped)
                    energy = lax.fori_loop(rest, rest + H, body, energy)
                else:
                    energy = lax.fori_loop(0, CX, body, energy, unroll=2)
                if step > 0 and damped:
                    note_energy(seen, step - 1, energy, norm)

    lane = lax.broadcasted_iota(jnp.int32, (1, LANES), 1)

    def inject(n, carry):
        code = table[4 + n]
        s, z, ly, lx = (code & 63, (code >> 6) & 255, (code >> 14) & 31, code >> 19)
        at = (lx + H, z >> 7, pl.ds(ly + LO, 1), slice(None))
        following[at] = following[at] + jnp.where(lane == (z & 127), amps[step * NSRC + s], 0.0)
        return carry

    lax.fori_loop(0, table[1], inject, 0)
    if step > 0:
        note_traces(current, seen, step - 1, table)


def join_kernel(last, *refs):
    if last:
        table, keep_x, keep_y, norm, speed, near_x, far_x, near_y, far_y, _, _ = refs[:11]
        field, seen, beside = refs[11:]
    else:
        speed, near_x, far_x, near_y, far_y, _, field = refs[:7]
        strips, beside = (refs[7:11], refs[11])
    gx, gy, edge_x, edge_y = place()
    mine_x, mine_y = odd()
    halo_x = [jnp.where(mine_x, near_x[...], far_x[...]), jnp.where(mine_x, far_x[...], near_x[...])]
    has = [
        (gx > 0).astype(jnp.float32),
        (gx < lax.axis_size(GX) - 1).astype(jnp.float32),
        (gy > 0).astype(jnp.float32),
        (gy < lax.axis_size(GY) - 1).astype(jnp.float32),
    ]
    low_x, high_x, low_y, high_y = [[e * m for e in second_coef] for m in has]
    beside[:, :, 4:8, :] = jnp.where(mine_y, near_y[...], far_y[...])
    beside[:, :, 8:16, :] = jnp.zeros((CX, 2, 8, LANES), jnp.float32)
    beside[:, :, 16:20, :] = jnp.where(mine_y, far_y[...], near_y[...])

    def ends(i):
        first, final = (0.0, 0.0)
        for k in range(1, 5):
            first = first + low_y[k - 1] * beside[i, :, 8 - k : 16 - k, :]
            final = final + high_y[k - 1] * beside[i, :, 8 + k : 16 + k, :]
        return first, final

    def inside(i, carry):
        first, final = ends(i)
        for at, extra in ((0, first), (16, final)):
            rows = slice(LO + at, LO + at + 8)
            field[i + H, :, rows, :] = (
                field[i + H, :, rows, :] + speed[i, :, at : at + 8, :] * extra
            )
        return carry

    lax.fori_loop(H, CX - H, inside, 0, unroll=4)
    for r in range(H):
        for i, coef, halo in ((r, low_x, halo_x[0]), (CX - H + r, high_x, halo_x[1])):
            across = 0.0
            for k in range(1, 5):
                at = H + i - k if i < H else i + k - CX
                if 0 <= at < H:
                    across = across + coef[k - 1] * halo[at]
            first, final = ends(i)
            for at, extra in ((0, first), (8, None), (16, final)):
                rows = slice(LO + at, LO + at + 8)
                part = across[:, at : at + 8, :]
                part = part if extra is None else part + extra
                field[i + H, :, rows, :] = (
                    field[i + H, :, rows, :] + speed[i, :, at : at + 8, :] * part
                )
    if not last:
        split_strips(field, mine_x, mine_y, *strips)
        return

    @pl.when(edge_x | edge_y)
    def _():
        add = lambda i, summed: summed + energy_row(field, i, keep_x, keep_y)
        zero = jnp.zeros((CY, LANES), jnp.float32)
        note_energy(seen, STEPS - 1, lax.fori_loop(0, CX, add, zero, unroll=4), norm)

    note_traces(field, seen, STEPS - 1, table)


def finish_kernel(field, pressure):
    for half in range(2):
        part = field[H : H + CX, half, INSIDE, :]
        pressure[:, :, half * LANES : (half + 1) * LANES] = part


def report_kernel(*refs):
    parts, (traces, energy) = (refs[:-2], refs[-2:])
    seen = parts[0][...]
    for part in parts[1:]:
        seen = seen + part[...]
    traces[...] = seen[:STEPS, :NREC]
    energy[...] = jnp.sum(seen[STEPS:].T, axis=0)


def vmem(count):
    return [pl.BlockSpec(memory_space=pltpu.VMEM)] * count


def smem(count):
    return [pl.BlockSpec(memory_space=pltpu.SMEM)] * count


def hbm(count):
    return [pl.BlockSpec(memory_space=pltpu.HBM)] * count


def shape(*sizes):
    return [jax.ShapeDtypeStruct(size, jnp.float32) for size in sizes]


def limit(mebibytes):
    return pltpu.CompilerParams(vmem_limit_bytes=mebibytes * 1024 * 1024)


def swap(strip, axis, far):
    size = lax.axis_size(axis)
    return lax.ppermute(strip, axis, [(i, (((i + far) ^ 1) - far) % size) for i in range(size)])


def exchange(strips):
    near_x, far_x, near_y, far_y = strips
    far_y = swap(far_y, GY, 1)
    far_x = swap(far_x, GX, 1)
    return (swap(near_x, GX, 0), far_x, swap(near_y, GY, 0), far_y)


def spread(value, by):
    columns = lax.axis_size(GY)
    pairs = []
    for gx in range(lax.axis_size(GX)):
        for gy in range(columns):
            pairs.append((gx * columns + gy, (gx ^ by[0]) * columns + (gy ^ by[1])))
    return lax.ppermute(value, BOTH, pairs)


def gather_sums(value):
    if (lax.axis_size(GX), lax.axis_size(GY)) != (8, 16):
        return [lax.psum(value, BOTH)]
    parts = [value, spread(value, (0, 1))]
    for flips in (((1, 0), (0, 2), (1, 2)), ((0, 4), (0, 8), (0, 12)), ((2, 0), (4, 0), (6, 0))):
        value = functools.reduce(jnp.add, parts)
        parts = [value] + [spread(value, by) for by in flips]
    return parts


def per_device(
    pressure,
    pressure_old,
    speed_term,
    layer_width,
    source_x,
    source_y,
    source_z,
    source_amp,
    receiver_x,
    receiver_y,
    receiver_z,
):
    stay = lambda value: pltpu.with_memory_space_constraint(value, pltpu.HBM)
    pressure, pressure_old, speed_term = [stay(v) for v in (pressure, pressure_old, speed_term)]
    small = [layer_width, source_x, source_y, source_z, receiver_x, receiver_y, receiver_z, source_amp.T]
    small = [stay(v) for v in small]
    staged = pltpu.VMEM(pressure.shape, jnp.float32)
    strips_out = shape(STRIP_X, STRIP_X, STRIP_Y, STRIP_Y)
    current, *strips = pl.pallas_call(
        pack_kernel,
        out_shape=shape(FIELD) + strips_out,
        in_specs=hbm(1),
        out_specs=vmem(5),
        scratch_shapes=[staged, pltpu.SemaphoreType.DMA((1, CHUNKS))],
        compiler_params=limit(8),
    )(pressure)
    previous, speed, *rest = pl.pallas_call(
        begin_kernel,
        out_shape=shape(FIELD, BLOCK, MEM_X, MEM_Y, BLOCK, BLOCK, SEEN, KEEP_X, KEEP_Y, NORM)
        + [
            jax.ShapeDtypeStruct((TABLE,), jnp.int32),
            jax.ShapeDtypeStruct((STEPS * NSRC,), jnp.float32),
        ],
        in_specs=hbm(10),
        out_specs=vmem(10) + smem(2),
        scratch_shapes=[staged, staged, pltpu.SemaphoreType.DMA((2, CHUNKS))]
        + [pltpu.SMEM((n,), jnp.int32) for n in (4, NSRC, NSRC, NSRC, NREC, NREC, NREC)]
        + [pltpu.SMEM((NSRC, STEPS), jnp.float32), pltpu.SemaphoreType.DMA((8,))],
        compiler_params=limit(8),
    )(*small, pressure_old, speed_term)
    state, keeps, table, amps = (rest[:5], rest[5:8], rest[8], rest[9])
    band = jnp.asarray(band_matrix())
    beside = pltpu.VMEM((CX, 2, 24, LANES), jnp.float32)
    for step in range(STEPS):
        halos = exchange(strips)
        following, *state = pl.pallas_call(
            functools.partial(inner_kernel, step),
            out_shape=shape(FIELD, MEM_X, MEM_Y, BLOCK, BLOCK, SEEN),
            in_specs=smem(2) + vmem(12),
            out_specs=vmem(6),
            scratch_shapes=[pltpu.VMEM(BLOCK, jnp.float32)],
            input_output_aliases={8: 0, 9: 1, 10: 2, 11: 3, 12: 4, 13: 5},
            compiler_params=limit(8),
        )(table, amps, band, current, speed, *keeps, previous, *state)
        previous = current
        if step < STEPS - 1:
            current, *strips = pl.pallas_call(
                functools.partial(join_kernel, False),
                out_shape=shape(FIELD) + strips_out,
                in_specs=vmem(6),
                out_specs=vmem(5),
                scratch_shapes=[beside],
                input_output_aliases={5: 0},
                compiler_params=limit(4),
            )(speed, *halos, following)
        else:
            current, seen = pl.pallas_call(
                functools.partial(join_kernel, True),
                out_shape=shape(FIELD, SEEN),
                in_specs=smem(1) + vmem(10),
                out_specs=vmem(2),
                scratch_shapes=[beside],
                input_output_aliases={9: 0, 10: 1},
                compiler_params=limit(4),
            )(table, *keeps, speed, *halos, following, state[-1])
    final = pl.pallas_call(
        finish_kernel,
        out_shape=jax.ShapeDtypeStruct(pressure.shape, jnp.float32),
        in_specs=vmem(1),
        out_specs=pl.BlockSpec(memory_space=pltpu.VMEM),
        compiler_params=limit(4),
    )(current)
    parts = gather_sums(seen)
    traces, energy = pl.pallas_call(
        report_kernel,
        out_shape=shape((STEPS, NREC), (STEPS,)),
        in_specs=vmem(len(parts)),
        out_specs=vmem(2),
        compiler_params=limit(2),
    )(*parts)
    return final, traces.T, energy


def solution(mesh):
    block = P(GX, GY, None)
    return jax.shard_map(
        per_device,
        mesh=mesh,
        in_specs=(block, block, block) + (P(),) * 8,
        out_specs=(block, P(), P()),
        check_vma=False,
    )
```

```python
import functools

import jax
import jax.numpy as jnp
import ml_dtypes
import numpy as np
from jax import lax
from jax.experimental import pallas as pl
from jax.experimental.pallas import tpu as pltpu
from jax.sharding import PartitionSpec as P

STEPS = 8
NSRC = 4
NREC = 64
NX = 192
NY = 384
NZ = 256
CX = 24
CY = 24
H = 4
LO = 8
LANES = 128
GX = "gx"
GY = "gy"
BOTH = (GX, GY)

first_coef = (0.8, -0.2, 4.0 / 105.0, -1.0 / 280.0)
second_coef = (1.6, -0.2, 8.0 / 315.0, -1.0 / 560.0)
centre_coef = -205.0 / 72.0
damping = 0.6

FIELD = (CX + 2 * H, 2, CY + 2 * LO, LANES)
MEM_X = (2, CX + 2 * H, 2, CY, LANES)
MEM_Y = (CX, 2, CY + 2 * LO, LANES)
BLOCK = (CX, 2, CY, LANES)
STRIP_X = (H, 2, CY, LANES)
STRIP_Y = (CX, 2, H, LANES)
SEEN = (2 * STEPS, LANES)
KEEP_X = (CX, CY, LANES)
KEEP_Y = (CY, LANES)
NORM = (1, LANES)
RECEIVERS = 8
TABLE = RECEIVERS + NREC
COMMON = 5040.0
CHUNKS = 4
INSIDE = slice(LO, LO + CY)


def band_matrix():
    band = np.zeros((NZ, NZ), np.float32)
    for k, tap in enumerate((8064.0, -1008.0, 128.0, -9.0)):
        band += tap * (np.eye(NZ, k=k + 1) + np.eye(NZ, k=-k - 1)).astype(np.float32)
    return np.concatenate([band, band], axis=0).astype(ml_dtypes.bfloat16)


def profile(position, low_width, high_width, length):
    inward_low = jnp.clip((low_width - position) / low_width, 0.0, 1.0)
    inward_high = jnp.clip((position - (length - 1 - high_width)) / high_width, 0.0, 1.0)
    return jnp.exp(-damping * (inward_low * inward_low + inward_high * inward_high))


def wide(value):
    return jnp.full((1, LANES), value, jnp.float32)


def keep_of(widths, start, dims, dim, length):
    position = start + lax.broadcasted_iota(jnp.int32, dims, dim)
    low, high = [jnp.full(dims, w, jnp.float32) for w in widths]
    return profile(position.astype(jnp.float32), low, high, length)


def whole_sum(widths, length):
    rows = -(-length // LANES)
    index = lax.broadcasted_iota(jnp.int32, (rows, LANES), 0) * LANES
    index = index + lax.broadcasted_iota(jnp.int32, (rows, LANES), 1)
    value = profile(index.astype(jnp.float32), wide(widths[0]), wide(widths[1]), length)
    return jnp.sum(jnp.where(index < length, value, 0.0))


def place():
    gx, gy = (lax.axis_index(GX), lax.axis_index(GY))
    edge_x = (gx == 0) | (gx == lax.axis_size(GX) - 1)
    edge_y = (gy == 0) | (gy == lax.axis_size(GY) - 1)
    return gx, gy, edge_x, edge_y


def energy_row(field, i, keep_x, keep_y):
    weight = 1.0 - keep_x[i] * keep_y[...]
    value = field[i + H, :, INSIDE, :]
    return weight * (value[0] * value[0] + value[1] * value[1])


def note_energy(seen, step, summed, norm):
    at = STEPS + step
    seen[at : at + 1, :] = jnp.sum(summed, axis=0, keepdims=True) / norm[...]


def note_traces(field, seen, step, table):
    lane = lax.broadcasted_iota(jnp.int32, (1, LANES), 1)

    def sample(n, carry):
        code = table[RECEIVERS + n]
        r, z, ly, lx = (code & 63, (code >> 6) & 255, (code >> 14) & 31, code >> 19)
        line = field[lx + H, z >> 7, pl.ds(ly + LO, 1), :]
        turned = pltpu.roll(line, (r - (z & 127)) & 127, axis=1)
        seen[step : step + 1, :] = jnp.where(lane == r, turned, seen[step : step + 1, :])
        return carry

    lax.fori_loop(0, table[0], sample, 0)


def fetch(pairs, sems):
    copies = []
    for n, (source, target) in enumerate(pairs):
        for c in range(CHUNKS):
            rows = pl.ds(c * (CX // CHUNKS), CX // CHUNKS)
            copies.append(pltpu.make_async_copy(source.at[rows], target.at[rows], sems.at[n, c]))
    for copy in copies:
        copy.start()
    return copies


def split_strips(field, mine_x, mine_y, near_x, far_y, far_x, near_y):
    rows = [field[CX : CX + H, :, INSIDE, :], field[H : 2 * H, :, INSIDE, :]]
    near_x[...] = jnp.where(mine_x, rows[1], rows[0])
    far_x[...] = jnp.where(mine_x, rows[0], rows[1])
    high, low = (LO + CY - H, LO)
    columns = [field[H : H + CX, :, at : at + H, :] for at in (high, low)]
    near_y[...] = jnp.where(mine_y, columns[1], columns[0])
    far_y[...] = jnp.where(mine_y, columns[0], columns[1])


def odd():
    return lax.axis_index(GX) % 2 == 1, lax.axis_index(GY) % 2 == 1


def pack_kernel(pressure, old, speed_term, field, near_x, far_y, far_x, near_y, raw_old, raw_speed, staged, sems):
    copies = fetch([(pressure, staged), (old, raw_old), (speed_term, raw_speed)], sems)
    field[...] = jnp.zeros(FIELD, jnp.float32)
    for copy in copies[:CHUNKS]:
        copy.wait()
    for half in range(2):
        part = staged[:, :, half * LANES : (half + 1) * LANES]
        field[H : H + CX, half, INSIDE, :] = part
    split_strips(field, *odd(), near_x, far_y, far_x, near_y)
    for copy in copies[CHUNKS:]:
        copy.wait()


def begin_kernel(
    widths_far, sx_far, sy_far, sz_far, rx_far, ry_far, rz_far, amp_far, raw_old, raw_speed,
    field, speed, memory_x, memory_y, zeta_x, zeta_y, seen, keep_x, keep_y, norm, table, amps,
    widths_ref, sx, sy, sz, rx, ry, rz, amp, small_sems,
):
    far = (widths_far, sx_far, sy_far, sz_far, rx_far, ry_far, rz_far, amp_far)
    near = (widths_ref, sx, sy, sz, rx, ry, rz, amp)
    small = [
        pltpu.make_async_copy(source, target, small_sems.at[n])
        for n, (source, target) in enumerate(zip(far, near))
    ]
    for copy in small:
        copy.start()
    gx, gy, edge_x, edge_y = place()
    start_x, start_y = (gx * CX, gy * CY)
    seen[...] = jnp.zeros(SEEN, jnp.float32)
    field[...] = jnp.zeros(FIELD, jnp.float32)
    for half in range(2):
        lanes = slice(half * LANES, (half + 1) * LANES)
        field[H : H + CX, half, INSIDE, :] = raw_old[:, :, lanes]
        speed[:, half, :, :] = raw_speed[:, :, lanes]

    @pl.when(edge_x)
    def _():
        memory_x[...] = jnp.zeros(MEM_X, jnp.float32)
        zeta_x[...] = jnp.zeros(BLOCK, jnp.float32)

    @pl.when(edge_y)
    def _():
        memory_y[...] = jnp.zeros(MEM_Y, jnp.float32)
        zeta_y[...] = jnp.zeros(BLOCK, jnp.float32)

    for copy in small:
        copy.wait()

    @pl.when(edge_x | edge_y)
    def _():
        widths = [widths_ref[n].astype(jnp.float32) for n in range(4)]
        keep = keep_of(widths[:2], start_x, KEEP_Y, 0, NX)
        for i in range(CX):
            keep_x[i] = jnp.broadcast_to(keep[i : i + 1], KEEP_Y)
        keep_y[...] = keep_of(widths[2:], start_y, KEEP_Y, 0, NY)
        cells = float(NX * NY) - whole_sum(widths[:2], NX) * whole_sum(widths[2:], NY)
        norm[...] = wide(float(NZ) * cells)

    def owned(px, py):
        lx, ly = (px - start_x, py - start_y)
        return lx, ly, (lx >= 0) & (lx < CX) & (ly >= 0) & (ly < CY)

    def note(at, n, px, py, pz):
        def add(r, count):
            lx, ly, here = owned(px[r], py[r])

            @pl.when(here)
            def _():
                table[at + count] = (((lx << 5) + ly) << 14) + (pz[r] << 6) + r

            return count + here.astype(jnp.int32)

        return lax.fori_loop(0, n, add, 0)

    table[0] = note(RECEIVERS, NREC, rx, ry, rz)
    table[1] = note(4, NSRC, sx, sy, sz)
    for t in range(STEPS):
        for n in range(NSRC):
            amps[t * NSRC + n] = amp[n, t]


def inner_kernel(
    step, table, amps, band, current, speed, keep_x, keep_y, norm,
    previous, memory_x_in, memory_y_in, zeta_x_in, zeta_y_in, seen_in,
    following, memory_x, memory_y, zeta_x, zeta_y, seen, bend_z,
):
    _, _, edge_x, edge_y = place()
    halves = [current[H : H + CX, h, INSIDE, :].reshape(CX * CY, LANES) for h in range(2)]
    whole = jnp.concatenate(halves, axis=1)
    high = whole.astype(jnp.bfloat16)
    low = (whole - high.astype(jnp.float32)).astype(jnp.bfloat16)
    bent = jnp.dot(
        jnp.concatenate([high, low], axis=1), band[...], preferred_element_type=jnp.float32
    )
    for h in range(2):
        bend_z[:, h, :, :] = bent[:, h * LANES : (h + 1) * LANES].reshape(CX, CY, LANES)
    source, target = (step % 2, 1 - step % 2)

    def taps(pick, want_first):
        second, first = (0.0, 0.0)
        for k in range(1, 5):
            up, down = (pick(k), pick(-k))
            second = second + second_coef[k - 1] * (up + down)
            if want_first:
                first = first + first_coef[k - 1] * (up - down)
        return second, first

    def first_only(pick):
        total = 0.0
        for k in range(1, 5):
            total = total + first_coef[k - 1] * (pick(k) - pick(-k))
        return total

    def row(in_x, in_y, damped, i, energy):
        for h in range(2):
            centre = current[i + H, h, INSIDE, :]
            second_x, grad_x = taps(lambda k: current[i + H + k, h, INSIDE, :], in_x)
            second_y, grad_y = taps(lambda k: current[i + H, h, LO + k : LO + CY + k, :], in_y)
            laplace = second_x + second_y + (3.0 * centre_coef) * centre
            laplace = laplace + bend_z[i, h] * (1.0 / COMMON)
            if in_x:
                keep = keep_x[i]
                take = keep - 1.0
                flux = first_only(lambda k: memory_x_in[source, i + H + k, h])
                bend = second_x + centre_coef * centre + flux
                zeta = keep * zeta_x_in[i, h] + take * bend
                zeta_x[i, h] = zeta
                laplace = laplace + (flux + zeta)
                memory_x[target, i + H, h] = keep * memory_x_in[source, i + H, h] + take * grad_x
            if in_y:
                keep = keep_y[...]
                take = keep - 1.0
                flux = first_only(lambda k: memory_y_in[i, h, LO + k : LO + CY + k, :])
                bend = second_y + centre_coef * centre + flux
                zeta = keep * zeta_y_in[i, h] + take * bend
                zeta_y[i, h] = zeta
                laplace = laplace + (flux + zeta)
                kept = keep * memory_y_in[i, h, INSIDE, :] + take * grad_y
                memory_y[i, h, INSIDE, :] = kept
            value = 2.0 * centre - previous[i + H, h, INSIDE, :]
            following[i + H, h, INSIDE, :] = value + speed[i, h] * laplace
            if step > 0 and damped:
                energy = energy + (1.0 - keep_x[i] * keep_y[...]) * (centre * centre)
        return energy

    for is_x in (False, True):
        for is_y in (False, True):

            @pl.when((edge_x == is_x) & (edge_y == is_y))
            def _():
                damped = is_x or is_y
                energy = jnp.zeros((CY, LANES), jnp.float32) if damped else 0
                body = functools.partial(row, is_x, is_y, damped)
                if is_x:
                    starts_low = lax.axis_index(GX) == 0
                    first = jnp.where(starts_low, 0, H)
                    energy = lax.fori_loop(first, first + CX - H, body, energy)
                    rest = jnp.where(starts_low, CX - H, 0)
                    body = functools.partial(row, False, is_y, damped)
                    energy = lax.fori_loop(rest, rest + H, body, energy)
                else:
                    energy = lax.fori_loop(0, CX, body, energy, unroll=2)
                if step > 0 and damped:
                    note_energy(seen, step - 1, energy, norm)

    lane = lax.broadcasted_iota(jnp.int32, (1, LANES), 1)

    def inject(n, carry):
        code = table[4 + n]
        s, z, ly, lx = (code & 63, (code >> 6) & 255, (code >> 14) & 31, code >> 19)
        at = (lx + H, z >> 7, pl.ds(ly + LO, 1), slice(None))
        following[at] = following[at] + jnp.where(lane == (z & 127), amps[step * NSRC + s], 0.0)
        return carry

    lax.fori_loop(0, table[1], inject, 0)
    if step > 0:
        note_traces(current, seen, step - 1, table)


def join_kernel(last, *refs):
    if last:
        table, keep_x, keep_y, norm, speed, near_x, far_y, far_x, near_y, _, _ = refs[:11]
        field, seen, beside = refs[11:]
    else:
        speed, near_x, far_y, far_x, near_y, _, field = refs[:7]
        strips, beside = (refs[7:11], refs[11])
    gx, gy, edge_x, edge_y = place()
    mine_x, mine_y = odd()
    halo_x = [jnp.where(mine_x, near_x[...], far_x[...]), jnp.where(mine_x, far_x[...], near_x[...])]
    has = [
        (gx > 0).astype(jnp.float32),
        (gx < lax.axis_size(GX) - 1).astype(jnp.float32),
        (gy > 0).astype(jnp.float32),
        (gy < lax.axis_size(GY) - 1).astype(jnp.float32),
    ]
    low_x, high_x, low_y, high_y = [[e * m for e in second_coef] for m in has]
    beside[:, :, 4:8, :] = jnp.where(mine_y, near_y[...], far_y[...])
    beside[:, :, 8:16, :] = jnp.zeros((CX, 2, 8, LANES), jnp.float32)
    beside[:, :, 16:20, :] = jnp.where(mine_y, far_y[...], near_y[...])

    def ends(i):
        first, final = (0.0, 0.0)
        for k in range(1, 5):
            first = first + low_y[k - 1] * beside[i, :, 8 - k : 16 - k, :]
            final = final + high_y[k - 1] * beside[i, :, 8 + k : 16 + k, :]
        return first, final

    def inside(i, carry):
        first, final = ends(i)
        for at, extra in ((0, first), (16, final)):
            rows = slice(LO + at, LO + at + 8)
            field[i + H, :, rows, :] = (
                field[i + H, :, rows, :] + speed[i, :, at : at + 8, :] * extra
            )
        return carry

    lax.fori_loop(H, CX - H, inside, 0, unroll=4)
    for r in range(H):
        for i, coef, halo in ((r, low_x, halo_x[0]), (CX - H + r, high_x, halo_x[1])):
            across = 0.0
            for k in range(1, 5):
                at = H + i - k if i < H else i + k - CX
                if 0 <= at < H:
                    across = across + coef[k - 1] * halo[at]
            first, final = ends(i)
            for at, extra in ((0, first), (8, None), (16, final)):
                rows = slice(LO + at, LO + at + 8)
                part = across[:, at : at + 8, :]
                part = part if extra is None else part + extra
                field[i + H, :, rows, :] = (
                    field[i + H, :, rows, :] + speed[i, :, at : at + 8, :] * part
                )
    if not last:
        split_strips(field, mine_x, mine_y, *strips)
        return

    @pl.when(edge_x | edge_y)
    def _():
        add = lambda i, summed: summed + energy_row(field, i, keep_x, keep_y)
        zero = jnp.zeros((CY, LANES), jnp.float32)
        note_energy(seen, STEPS - 1, lax.fori_loop(0, CX, add, zero, unroll=4), norm)

    note_traces(field, seen, STEPS - 1, table)


def finish_kernel(field, pressure):
    for half in range(2):
        part = field[H : H + CX, half, INSIDE, :]
        pressure[:, :, half * LANES : (half + 1) * LANES] = part


def report_kernel(*refs):
    parts, (traces, energy) = (refs[:-2], refs[-2:])
    seen = parts[0][...]
    for part in parts[1:]:
        seen = seen + part[...]
    traces[...] = seen[:STEPS, :NREC]
    energy[...] = jnp.sum(seen[STEPS:].T, axis=0)


def vmem(count):
    return [pl.BlockSpec(memory_space=pltpu.VMEM)] * count


def smem(count):
    return [pl.BlockSpec(memory_space=pltpu.SMEM)] * count


def hbm(count):
    return [pl.BlockSpec(memory_space=pltpu.HBM)] * count


def shape(*sizes):
    return [jax.ShapeDtypeStruct(size, jnp.float32) for size in sizes]


def limit(mebibytes):
    return pltpu.CompilerParams(vmem_limit_bytes=mebibytes * 1024 * 1024)


def swap(strip, axis, far):
    size = lax.axis_size(axis)
    return lax.ppermute(strip, axis, [(i, (((i + far) ^ 1) - far) % size) for i in range(size)])


def exchange(strips):
    near_x, far_y, far_x, near_y = strips
    return (swap(near_x, GX, 0), swap(far_y, GY, 1), swap(far_x, GX, 1), swap(near_y, GY, 0))


def spread(value, by):
    columns = lax.axis_size(GY)
    pairs = []
    for gx in range(lax.axis_size(GX)):
        for gy in range(columns):
            pairs.append((gx * columns + gy, (gx ^ by[0]) * columns + (gy ^ by[1])))
    return lax.ppermute(value, BOTH, pairs)


def gather_sums(value):
    if (lax.axis_size(GX), lax.axis_size(GY)) != (8, 16):
        return [lax.psum(value, BOTH)]
    parts = [value, spread(value, (0, 1))]
    for flips in (((1, 0), (0, 2), (1, 2)), ((0, 4), (0, 8), (0, 12)), ((2, 0), (4, 0), (6, 0))):
        value = functools.reduce(jnp.add, parts)
        parts = [value] + [spread(value, by) for by in flips]
    return parts


def per_device(
    pressure,
    pressure_old,
    speed_term,
    layer_width,
    source_x,
    source_y,
    source_z,
    source_amp,
    receiver_x,
    receiver_y,
    receiver_z,
):
    stay = lambda value: pltpu.with_memory_space_constraint(value, pltpu.HBM)
    pressure, pressure_old, speed_term = [stay(v) for v in (pressure, pressure_old, speed_term)]
    small = [layer_width, source_x, source_y, source_z, receiver_x, receiver_y, receiver_z, source_amp.T]
    small = [stay(v) for v in small]
    staged = pltpu.VMEM(pressure.shape, jnp.float32)
    strips_out = shape(STRIP_X, STRIP_Y, STRIP_X, STRIP_Y)
    current, *strips, raw_old, raw_speed = pl.pallas_call(
        pack_kernel,
        out_shape=shape(FIELD) + strips_out + shape(pressure.shape, pressure.shape),
        in_specs=hbm(3),
        out_specs=vmem(7),
        scratch_shapes=[staged, pltpu.SemaphoreType.DMA((3, CHUNKS))],
        compiler_params=limit(8),
    )(pressure, pressure_old, speed_term)
    previous, speed, *rest = pl.pallas_call(
        begin_kernel,
        out_shape=shape(FIELD, BLOCK, MEM_X, MEM_Y, BLOCK, BLOCK, SEEN, KEEP_X, KEEP_Y, NORM)
        + [
            jax.ShapeDtypeStruct((TABLE,), jnp.int32),
            jax.ShapeDtypeStruct((STEPS * NSRC,), jnp.float32),
        ],
        in_specs=hbm(8) + vmem(2),
        out_specs=vmem(10) + smem(2),
        scratch_shapes=[pltpu.SMEM((n,), jnp.int32) for n in (4, NSRC, NSRC, NSRC, NREC, NREC, NREC)]
        + [pltpu.SMEM((NSRC, STEPS), jnp.float32), pltpu.SemaphoreType.DMA((8,))],
        compiler_params=limit(8),
    )(*small, raw_old, raw_speed)
    state, keeps, table, amps = (rest[:5], rest[5:8], rest[8], rest[9])
    band = jnp.asarray(band_matrix())
    beside = pltpu.VMEM((CX, 2, 24, LANES), jnp.float32)
    for step in range(STEPS):
        halos = exchange(strips)
        following, *state = pl.pallas_call(
            functools.partial(inner_kernel, step),
            out_shape=shape(FIELD, MEM_X, MEM_Y, BLOCK, BLOCK, SEEN),
            in_specs=smem(2) + vmem(12),
            out_specs=vmem(6),
            scratch_shapes=[pltpu.VMEM(BLOCK, jnp.float32)],
            input_output_aliases={8: 0, 9: 1, 10: 2, 11: 3, 12: 4, 13: 5},
            compiler_params=limit(8),
        )(table, amps, band, current, speed, *keeps, previous, *state)
        previous = current
        if step < STEPS - 1:
            current, *strips = pl.pallas_call(
                functools.partial(join_kernel, False),
                out_shape=shape(FIELD) + strips_out,
                in_specs=vmem(6),
                out_specs=vmem(5),
                scratch_shapes=[beside],
                input_output_aliases={5: 0},
                compiler_params=limit(4),
            )(speed, *halos, following)
        else:
            current, seen = pl.pallas_call(
                functools.partial(join_kernel, True),
                out_shape=shape(FIELD, SEEN),
                in_specs=smem(1) + vmem(10),
                out_specs=vmem(2),
                scratch_shapes=[beside],
                input_output_aliases={9: 0, 10: 1},
                compiler_params=limit(4),
            )(table, *keeps, speed, *halos, following, state[-1])
    final = pl.pallas_call(
        finish_kernel,
        out_shape=jax.ShapeDtypeStruct(pressure.shape, jnp.float32),
        in_specs=vmem(1),
        out_specs=pl.BlockSpec(memory_space=pltpu.VMEM),
        compiler_params=limit(4),
    )(current)
    parts = gather_sums(seen)
    traces, energy = pl.pallas_call(
        report_kernel,
        out_shape=shape((STEPS, NREC), (STEPS,)),
        in_specs=vmem(len(parts)),
        out_specs=vmem(2),
        compiler_params=limit(2),
    )(*parts)
    return final, traces.T, energy


def solution(mesh):
    block = P(GX, GY, None)
    return jax.shard_map(
        per_device,
        mesh=mesh,
        in_specs=(block, block, block) + (P(),) * 8,
        out_specs=(block, P(), P()),
        check_vma=False,
    )
```

```python
import functools

import jax
import jax.numpy as jnp
import ml_dtypes
import numpy as np
from jax import lax
from jax.experimental import pallas as pl
from jax.experimental.pallas import tpu as pltpu
from jax.sharding import PartitionSpec as P

STEPS = 8
NSRC = 4
NREC = 64
NX = 192
NY = 384
NZ = 256
CX = 24
CY = 24
H = 4
LO = 8
LANES = 128
GX = "gx"
GY = "gy"
BOTH = (GX, GY)

first_coef = (0.8, -0.2, 4.0 / 105.0, -1.0 / 280.0)
second_coef = (1.6, -0.2, 8.0 / 315.0, -1.0 / 560.0)
centre_coef = -205.0 / 72.0
damping = 0.6

FIELD = (CX + 2 * H, 2, CY + 2 * LO, LANES)
MEM_X = (2, CX + 2 * H, 2, CY, LANES)
MEM_Y = (CX, 2, CY + 2 * LO, LANES)
BLOCK = (CX, 2, CY, LANES)
STRIP_X = (H, 2, CY, LANES)
STRIP_Y = (CX, 2, H, LANES)
SEEN = (2 * STEPS, LANES)
KEEP_X = (CX, CY, LANES)
KEEP_Y = (CY, LANES)
NORM = (1, LANES)
RECEIVERS = 12
TABLE = RECEIVERS + NREC + 1
COMMON = 5040.0
CHUNKS = 4
INSIDE = slice(LO, LO + CY)


def band_matrix():
    band = np.zeros((NZ, NZ), np.float32)
    for k, tap in enumerate((8064.0, -1008.0, 128.0, -9.0)):
        band += tap * (np.eye(NZ, k=k + 1) + np.eye(NZ, k=-k - 1)).astype(np.float32)
    return np.concatenate([band, band], axis=0).astype(ml_dtypes.bfloat16)


def profile(position, low_width, high_width, length):
    inward_low = jnp.clip((low_width - position) / low_width, 0.0, 1.0)
    inward_high = jnp.clip((position - (length - 1 - high_width)) / high_width, 0.0, 1.0)
    return jnp.exp(-damping * (inward_low * inward_low + inward_high * inward_high))


def wide(value):
    return jnp.full((1, LANES), value, jnp.float32)


def keep_of(widths, start, dims, dim, length):
    position = start + lax.broadcasted_iota(jnp.int32, dims, dim)
    low, high = [jnp.full(dims, w, jnp.float32) for w in widths]
    return profile(position.astype(jnp.float32), low, high, length)


def whole_sum(widths, length):
    rows = -(-length // LANES)
    index = lax.broadcasted_iota(jnp.int32, (rows, LANES), 0) * LANES
    index = index + lax.broadcasted_iota(jnp.int32, (rows, LANES), 1)
    value = profile(index.astype(jnp.float32), wide(widths[0]), wide(widths[1]), length)
    return jnp.sum(jnp.where(index < length, value, 0.0))


def place():
    gx, gy = (lax.axis_index(GX), lax.axis_index(GY))
    edge_x = (gx == 0) | (gx == lax.axis_size(GX) - 1)
    edge_y = (gy == 0) | (gy == lax.axis_size(GY) - 1)
    return gx, gy, edge_x, edge_y


def energy_row(field, i, keep_x, keep_y):
    weight = 1.0 - keep_x[i] * keep_y[...]
    value = field[i + H, :, INSIDE, :]
    return weight * (value[0] * value[0] + value[1] * value[1])


def note_energy(seen, step, summed, norm):
    at = STEPS + step
    seen[at : at + 1, :] = jnp.sum(summed, axis=0, keepdims=True) / norm[...]


def note_traces(field, seen, step, table):
    lane = lax.broadcasted_iota(jnp.int32, (1, LANES), 1)

    def sample(n, carry):
        code = table[RECEIVERS + n]
        r, z, ly, lx = (code & 63, (code >> 6) & 255, (code >> 14) & 31, code >> 19)
        line = field[lx + H, z >> 7, pl.ds(ly + LO, 1), :]
        turned = pltpu.roll(line, (r - (z & 127)) & 127, axis=1)
        seen[step : step + 1, :] = jnp.where(lane == r, turned, seen[step : step + 1, :])
        return carry

    lax.fori_loop(0, table[0], sample, 0)


def fetch(pairs, sems):
    copies = []
    for n, (source, target) in enumerate(pairs):
        for c in range(CHUNKS):
            rows = pl.ds(c * (CX // CHUNKS), CX // CHUNKS)
            copies.append(pltpu.make_async_copy(source.at[rows], target.at[rows], sems.at[n, c]))
    for copy in copies:
        copy.start()
    return copies


def split_strips(field, mine_x, mine_y, near_x, far_y, far_x, near_y):
    rows = [field[CX : CX + H, :, INSIDE, :], field[H : 2 * H, :, INSIDE, :]]
    near_x[...] = jnp.where(mine_x, rows[1], rows[0])
    far_x[...] = jnp.where(mine_x, rows[0], rows[1])
    high, low = (LO + CY - H, LO)
    columns = [field[H : H + CX, :, at : at + H, :] for at in (high, low)]
    near_y[...] = jnp.where(mine_y, columns[1], columns[0])
    far_y[...] = jnp.where(mine_y, columns[0], columns[1])


def odd():
    return lax.axis_index(GX) % 2 == 1, lax.axis_index(GY) % 2 == 1


def pack_kernel(pressure, old, speed_term, field, near_x, far_y, far_x, near_y, raw_old, raw_speed, staged, sems):
    copies = fetch([(pressure, staged), (old, raw_old), (speed_term, raw_speed)], sems)
    field[...] = jnp.zeros(FIELD, jnp.float32)
    for copy in copies[:CHUNKS]:
        copy.wait()
    for half in range(2):
        part = staged[:, :, half * LANES : (half + 1) * LANES]
        field[H : H + CX, half, INSIDE, :] = part
    split_strips(field, *odd(), near_x, far_y, far_x, near_y)
    for copy in copies[CHUNKS:]:
        copy.wait()


def begin_kernel(
    widths_far, sx_far, sy_far, sz_far, rx_far, ry_far, rz_far, amp_far, raw_old, raw_speed,
    field, speed, memory_x, memory_y, zeta_x, zeta_y, seen, keep_x, keep_y, norm, table, amps,
    widths_ref, sx, sy, sz, rx, ry, rz, amp, small_sems,
):
    far = (widths_far, sx_far, sy_far, sz_far, rx_far, ry_far, rz_far, amp_far)
    near = (widths_ref, sx, sy, sz, rx, ry, rz, amp)
    small = [
        pltpu.make_async_copy(source, target, small_sems.at[n])
        for n, (source, target) in enumerate(zip(far, near))
    ]
    for copy in small:
        copy.start()
    gx, gy, edge_x, edge_y = place()
    start_x, start_y = (gx * CX, gy * CY)
    seen[...] = jnp.zeros(SEEN, jnp.float32)
    field[...] = jnp.zeros(FIELD, jnp.float32)
    for half in range(2):
        lanes = slice(half * LANES, (half + 1) * LANES)
        field[H : H + CX, half, INSIDE, :] = raw_old[:, :, lanes]
        speed[:, half, :, :] = raw_speed[:, :, lanes]

    @pl.when(edge_x)
    def _():
        memory_x[...] = jnp.zeros(MEM_X, jnp.float32)
        zeta_x[...] = jnp.zeros(BLOCK, jnp.float32)

    @pl.when(edge_y)
    def _():
        memory_y[...] = jnp.zeros(MEM_Y, jnp.float32)
        zeta_y[...] = jnp.zeros(BLOCK, jnp.float32)

    for copy in small:
        copy.wait()

    @pl.when(edge_x | edge_y)
    def _():
        widths = [widths_ref[n].astype(jnp.float32) for n in range(4)]
        keep = keep_of(widths[:2], start_x, KEEP_Y, 0, NX)
        for i in range(CX):
            keep_x[i] = jnp.broadcast_to(keep[i : i + 1], KEEP_Y)
        keep_y[...] = keep_of(widths[2:], start_y, KEEP_Y, 0, NY)
        cells = float(NX * NY) - whole_sum(widths[:2], NX) * whole_sum(widths[2:], NY)
        norm[...] = wide(float(NZ) * cells)

    def owned(px, py):
        lx, ly = (px - start_x, py - start_y)
        return lx, ly, (lx >= 0) & (lx < CX) & (ly >= 0) & (ly < CY)

    def note(at, n, px, py, pz):
        def add(r, count):
            lx, ly, here = owned(px[r], py[r])
            table[at + count] = (((lx << 5) + ly) << 14) + (pz[r] << 6) + r
            return count + here.astype(jnp.int32)

        return lax.fori_loop(0, n, add, 0, unroll=4)

    table[0] = note(RECEIVERS, NREC, rx, ry, rz)
    table[1] = note(4, NSRC, sx, sy, sz)
    for t in range(STEPS):
        for n in range(NSRC):
            amps[t * NSRC + n] = amp[n, t]


def inner_kernel(
    step, table, amps, band, current, speed, keep_x, keep_y, norm,
    previous, memory_x_in, memory_y_in, zeta_x_in, zeta_y_in, seen_in,
    following, memory_x, memory_y, zeta_x, zeta_y, seen, bend_z,
):
    _, _, edge_x, edge_y = place()
    halves = [current[H : H + CX, h, INSIDE, :].reshape(CX * CY, LANES) for h in range(2)]
    whole = jnp.concatenate(halves, axis=1)
    high = whole.astype(jnp.bfloat16)
    low = (whole - high.astype(jnp.float32)).astype(jnp.bfloat16)
    bent = jnp.dot(
        jnp.concatenate([high, low], axis=1), band[...], preferred_element_type=jnp.float32
    )
    for h in range(2):
        bend_z[:, h, :, :] = bent[:, h * LANES : (h + 1) * LANES].reshape(CX, CY, LANES)
    source, target = (step % 2, 1 - step % 2)

    def taps(pick, want_first):
        second, first = (0.0, 0.0)
        for k in range(1, 5):
            up, down = (pick(k), pick(-k))
            second = second + second_coef[k - 1] * (up + down)
            if want_first:
                first = first + first_coef[k - 1] * (up - down)
        return second, first

    def first_only(pick):
        total = 0.0
        for k in range(1, 5):
            total = total + first_coef[k - 1] * (pick(k) - pick(-k))
        return total

    def row(in_x, in_y, damped, i, energy):
        for h in range(2):
            centre = current[i + H, h, INSIDE, :]
            second_x, grad_x = taps(lambda k: current[i + H + k, h, INSIDE, :], in_x)
            second_y, grad_y = taps(lambda k: current[i + H, h, LO + k : LO + CY + k, :], in_y)
            laplace = second_x + second_y + (3.0 * centre_coef) * centre
            laplace = laplace + bend_z[i, h] * (1.0 / COMMON)
            if in_x:
                keep = keep_x[i]
                take = keep - 1.0
                flux = first_only(lambda k: memory_x_in[source, i + H + k, h])
                bend = second_x + centre_coef * centre + flux
                zeta = keep * zeta_x_in[i, h] + take * bend
                zeta_x[i, h] = zeta
                laplace = laplace + (flux + zeta)
                memory_x[target, i + H, h] = keep * memory_x_in[source, i + H, h] + take * grad_x
            if in_y:
                keep = keep_y[...]
                take = keep - 1.0
                flux = first_only(lambda k: memory_y_in[i, h, LO + k : LO + CY + k, :])
                bend = second_y + centre_coef * centre + flux
                zeta = keep * zeta_y_in[i, h] + take * bend
                zeta_y[i, h] = zeta
                laplace = laplace + (flux + zeta)
                kept = keep * memory_y_in[i, h, INSIDE, :] + take * grad_y
                memory_y[i, h, INSIDE, :] = kept
            value = 2.0 * centre - previous[i + H, h, INSIDE, :]
            following[i + H, h, INSIDE, :] = value + speed[i, h] * laplace
            if step > 0 and damped:
                energy = energy + (1.0 - keep_x[i] * keep_y[...]) * (centre * centre)
        return energy

    for is_x in (False, True):
        for is_y in (False, True):

            @pl.when((edge_x == is_x) & (edge_y == is_y))
            def _():
                damped = is_x or is_y
                energy = jnp.zeros((CY, LANES), jnp.float32) if damped else 0
                body = functools.partial(row, is_x, is_y, damped)
                if is_x:
                    starts_low = lax.axis_index(GX) == 0
                    first = jnp.where(starts_low, 0, H)
                    energy = lax.fori_loop(first, first + CX - H, body, energy)
                    rest = jnp.where(starts_low, CX - H, 0)
                    body = functools.partial(row, False, is_y, damped)
                    energy = lax.fori_loop(rest, rest + H, body, energy)
                else:
                    energy = lax.fori_loop(0, CX, body, energy, unroll=2)
                if step > 0 and damped:
                    note_energy(seen, step - 1, energy, norm)

    lane = lax.broadcasted_iota(jnp.int32, (1, LANES), 1)

    def inject(n, carry):
        code = table[4 + n]
        s, z, ly, lx = (code & 63, (code >> 6) & 255, (code >> 14) & 31, code >> 19)
        at = (lx + H, z >> 7, pl.ds(ly + LO, 1), slice(None))
        following[at] = following[at] + jnp.where(lane == (z & 127), amps[step * NSRC + s], 0.0)
        return carry

    lax.fori_loop(0, table[1], inject, 0)
    if step > 0:
        note_traces(current, seen, step - 1, table)


def join_kernel(last, *refs):
    if last:
        table, keep_x, keep_y, norm, speed, near_x, far_y, far_x, near_y, _, _ = refs[:11]
        field, seen, beside = refs[11:]
    else:
        speed, near_x, far_y, far_x, near_y, _, field = refs[:7]
        strips, beside = (refs[7:11], refs[11])
    gx, gy, edge_x, edge_y = place()
    mine_x, mine_y = odd()
    halo_x = [jnp.where(mine_x, near_x[...], far_x[...]), jnp.where(mine_x, far_x[...], near_x[...])]
    has = [
        (gx > 0).astype(jnp.float32),
        (gx < lax.axis_size(GX) - 1).astype(jnp.float32),
        (gy > 0).astype(jnp.float32),
        (gy < lax.axis_size(GY) - 1).astype(jnp.float32),
    ]
    low_x, high_x, low_y, high_y = [[e * m for e in second_coef] for m in has]
    beside[:, :, 4:8, :] = jnp.where(mine_y, near_y[...], far_y[...])
    beside[:, :, 8:16, :] = jnp.zeros((CX, 2, 8, LANES), jnp.float32)
    beside[:, :, 16:20, :] = jnp.where(mine_y, far_y[...], near_y[...])

    def ends(i):
        first, final = (0.0, 0.0)
        for k in range(1, 5):
            first = first + low_y[k - 1] * beside[i, :, 8 - k : 16 - k, :]
            final = final + high_y[k - 1] * beside[i, :, 8 + k : 16 + k, :]
        return first, final

    def inside(i, carry):
        first, final = ends(i)
        for at, extra in ((0, first), (16, final)):
            rows = slice(LO + at, LO + at + 8)
            field[i + H, :, rows, :] = (
                field[i + H, :, rows, :] + speed[i, :, at : at + 8, :] * extra
            )
        return carry

    lax.fori_loop(H, CX - H, inside, 0, unroll=4)
    for r in range(H):
        for i, coef, halo in ((r, low_x, halo_x[0]), (CX - H + r, high_x, halo_x[1])):
            across = 0.0
            for k in range(1, 5):
                at = H + i - k if i < H else i + k - CX
                if 0 <= at < H:
                    across = across + coef[k - 1] * halo[at]
            first, final = ends(i)
            for at, extra in ((0, first), (8, None), (16, final)):
                rows = slice(LO + at, LO + at + 8)
                part = across[:, at : at + 8, :]
                part = part if extra is None else part + extra
                field[i + H, :, rows, :] = (
                    field[i + H, :, rows, :] + speed[i, :, at : at + 8, :] * part
                )
    if not last:
        split_strips(field, mine_x, mine_y, *strips)
        return

    @pl.when(edge_x | edge_y)
    def _():
        add = lambda i, summed: summed + energy_row(field, i, keep_x, keep_y)
        zero = jnp.zeros((CY, LANES), jnp.float32)
        note_energy(seen, STEPS - 1, lax.fori_loop(0, CX, add, zero, unroll=4), norm)

    note_traces(field, seen, STEPS - 1, table)


def finish_kernel(field, pressure):
    for half in range(2):
        part = field[H : H + CX, half, INSIDE, :]
        pressure[:, :, half * LANES : (half + 1) * LANES] = part


def report_kernel(*refs):
    parts, (traces, energy) = (refs[:-2], refs[-2:])
    seen = parts[0][...]
    for part in parts[1:]:
        seen = seen + part[...]
    traces[...] = seen[:STEPS, :NREC]
    energy[...] = jnp.sum(seen[STEPS:].T, axis=0)


def vmem(count):
    return [pl.BlockSpec(memory_space=pltpu.VMEM)] * count


def smem(count):
    return [pl.BlockSpec(memory_space=pltpu.SMEM)] * count


def hbm(count):
    return [pl.BlockSpec(memory_space=pltpu.HBM)] * count


def shape(*sizes):
    return [jax.ShapeDtypeStruct(size, jnp.float32) for size in sizes]


def limit(mebibytes):
    return pltpu.CompilerParams(vmem_limit_bytes=mebibytes * 1024 * 1024)


def swap(strip, axis, far):
    rows, columns = (lax.axis_size(GX), lax.axis_size(GY))
    pairs = []
    for gx in range(rows):
        for gy in range(columns):
            to_x = ((gx + far) ^ 1) - far if axis == GX else gx
            to_y = ((gy + far) ^ 1) - far if axis == GY else gy
            if not 0 <= to_x < rows:
                to_x, to_y = (gx, gy ^ 1)
            if not 0 <= to_y < columns:
                to_x, to_y = (gx ^ 1, gy)
            pairs.append((gx * columns + gy, to_x * columns + to_y))
    return lax.ppermute(strip, BOTH, pairs)


def exchange(strips):
    near_x, far_y, far_x, near_y = strips
    return (swap(near_x, GX, 0), swap(far_y, GY, 1), swap(far_x, GX, 1), swap(near_y, GY, 0))


def spread(value, by):
    columns = lax.axis_size(GY)
    pairs = []
    for gx in range(lax.axis_size(GX)):
        for gy in range(columns):
            pairs.append((gx * columns + gy, (gx ^ by[0]) * columns + (gy ^ by[1])))
    return lax.ppermute(value, BOTH, pairs)


def gather_sums(value):
    if (lax.axis_size(GX), lax.axis_size(GY)) != (8, 16):
        return [lax.psum(value, BOTH)]
    parts = [value, spread(value, (0, 1))]
    for flips in (((1, 0), (0, 2), (1, 2)), ((0, 4), (0, 8), (0, 12)), ((2, 0), (4, 0), (6, 0))):
        value = functools.reduce(jnp.add, parts)
        parts = [value] + [spread(value, by) for by in flips]
    return parts


def per_device(
    pressure,
    pressure_old,
    speed_term,
    layer_width,
    source_x,
    source_y,
    source_z,
    source_amp,
    receiver_x,
    receiver_y,
    receiver_z,
):
    stay = lambda value: pltpu.with_memory_space_constraint(value, pltpu.HBM)
    pressure, pressure_old, speed_term = [stay(v) for v in (pressure, pressure_old, speed_term)]
    small = [layer_width, source_x, source_y, source_z, receiver_x, receiver_y, receiver_z, source_amp.T]
    small = [stay(v) for v in small]
    staged = pltpu.VMEM(pressure.shape, jnp.float32)
    strips_out = shape(STRIP_X, STRIP_Y, STRIP_X, STRIP_Y)
    current, *strips, raw_old, raw_speed = pl.pallas_call(
        pack_kernel,
        out_shape=shape(FIELD) + strips_out + shape(pressure.shape, pressure.shape),
        in_specs=hbm(3),
        out_specs=vmem(7),
        scratch_shapes=[staged, pltpu.SemaphoreType.DMA((3, CHUNKS))],
        compiler_params=limit(8),
    )(pressure, pressure_old, speed_term)
    previous, speed, *rest = pl.pallas_call(
        begin_kernel,
        out_shape=shape(FIELD, BLOCK, MEM_X, MEM_Y, BLOCK, BLOCK, SEEN, KEEP_X, KEEP_Y, NORM)
        + [
            jax.ShapeDtypeStruct((TABLE,), jnp.int32),
            jax.ShapeDtypeStruct((STEPS * NSRC,), jnp.float32),
        ],
        in_specs=hbm(8) + vmem(2),
        out_specs=vmem(10) + smem(2),
        scratch_shapes=[pltpu.SMEM((n,), jnp.int32) for n in (4, NSRC, NSRC, NSRC, NREC, NREC, NREC)]
        + [pltpu.SMEM((NSRC, STEPS), jnp.float32), pltpu.SemaphoreType.DMA((8,))],
        compiler_params=limit(8),
    )(*small, raw_old, raw_speed)
    state, keeps, table, amps = (rest[:5], rest[5:8], rest[8], rest[9])
    band = jnp.asarray(band_matrix())
    beside = pltpu.VMEM((CX, 2, 24, LANES), jnp.float32)
    for step in range(STEPS):
        halos = exchange(strips)
        following, *state = pl.pallas_call(
            functools.partial(inner_kernel, step),
            out_shape=shape(FIELD, MEM_X, MEM_Y, BLOCK, BLOCK, SEEN),
            in_specs=smem(2) + vmem(12),
            out_specs=vmem(6),
            scratch_shapes=[pltpu.VMEM(BLOCK, jnp.float32)],
            input_output_aliases={8: 0, 9: 1, 10: 2, 11: 3, 12: 4, 13: 5},
            compiler_params=limit(8),
        )(table, amps, band, current, speed, *keeps, previous, *state)
        previous = current
        if step < STEPS - 1:
            current, *strips = pl.pallas_call(
                functools.partial(join_kernel, False),
                out_shape=shape(FIELD) + strips_out,
                in_specs=vmem(6),
                out_specs=vmem(5),
                scratch_shapes=[beside],
                input_output_aliases={5: 0},
                compiler_params=limit(4),
            )(speed, *halos, following)
        else:
            current, seen = pl.pallas_call(
                functools.partial(join_kernel, True),
                out_shape=shape(FIELD, SEEN),
                in_specs=smem(1) + vmem(10),
                out_specs=vmem(2),
                scratch_shapes=[beside],
                input_output_aliases={9: 0, 10: 1},
                compiler_params=limit(4),
            )(table, *keeps, speed, *halos, following, state[-1])
    final = pl.pallas_call(
        finish_kernel,
        out_shape=jax.ShapeDtypeStruct(pressure.shape, jnp.float32),
        in_specs=vmem(1),
        out_specs=pl.BlockSpec(memory_space=pltpu.VMEM),
        compiler_params=limit(4),
    )(current)
    parts = gather_sums(seen)
    traces, energy = pl.pallas_call(
        report_kernel,
        out_shape=shape((STEPS, NREC), (STEPS,)),
        in_specs=vmem(len(parts)),
        out_specs=vmem(2),
        compiler_params=limit(2),
    )(*parts)
    return final, traces.T, energy


def solution(mesh):
    block = P(GX, GY, None)
    return jax.shard_map(
        per_device,
        mesh=mesh,
        in_specs=(block, block, block) + (P(),) * 8,
        out_specs=(block, P(), P()),
        check_vma=False,
    )
```

```python
import functools

import jax
import jax.numpy as jnp
import ml_dtypes
import numpy as np
from jax import lax
from jax.experimental import pallas as pl
from jax.experimental.pallas import tpu as pltpu
from jax.sharding import PartitionSpec as P

STEPS = 8
NSRC = 4
NREC = 64
NX = 192
NY = 384
NZ = 256
CX = 24
CY = 24
H = 4
LO = 8
LANES = 128
GX = "gx"
GY = "gy"
BOTH = (GX, GY)

first_coef = (0.8, -0.2, 4.0 / 105.0, -1.0 / 280.0)
second_coef = (1.6, -0.2, 8.0 / 315.0, -1.0 / 560.0)
centre_coef = -205.0 / 72.0
damping = 0.6

FIELD = (CX + 2 * H, 2, CY + 2 * LO, LANES)
MEM_X = (2, CX + 2 * H, 2, CY, LANES)
MEM_Y = (CX, 2, CY + 2 * LO, LANES)
BLOCK = (CX, 2, CY, LANES)
STRIP_X = (H, 2, CY, LANES)
STRIP_Y = (CX, 2, H, LANES)
SEEN = (2 * STEPS, LANES)
KEEP_X = (CX, CY, LANES)
KEEP_Y = (CY, LANES)
NORM = (1, LANES)
RECEIVERS = 12
TABLE = RECEIVERS + NREC + 1
COMMON = 5040.0
CHUNKS = 4
INSIDE = slice(LO, LO + CY)


def band_matrix():
    band = np.zeros((NZ, NZ), np.float32)
    for k, tap in enumerate((8064.0, -1008.0, 128.0, -9.0)):
        band += tap * (np.eye(NZ, k=k + 1) + np.eye(NZ, k=-k - 1)).astype(np.float32)
    return np.concatenate([band, band], axis=0).astype(ml_dtypes.bfloat16)


def profile(position, low_width, high_width, length):
    inward_low = jnp.clip((low_width - position) / low_width, 0.0, 1.0)
    inward_high = jnp.clip((position - (length - 1 - high_width)) / high_width, 0.0, 1.0)
    return jnp.exp(-damping * (inward_low * inward_low + inward_high * inward_high))


def wide(value):
    return jnp.full((1, LANES), value, jnp.float32)


def keep_of(widths, start, dims, dim, length):
    position = start + lax.broadcasted_iota(jnp.int32, dims, dim)
    low, high = [jnp.full(dims, w, jnp.float32) for w in widths]
    return profile(position.astype(jnp.float32), low, high, length)


def whole_sum(widths, length):
    rows = -(-length // LANES)
    index = lax.broadcasted_iota(jnp.int32, (rows, LANES), 0) * LANES
    index = index + lax.broadcasted_iota(jnp.int32, (rows, LANES), 1)
    value = profile(index.astype(jnp.float32), wide(widths[0]), wide(widths[1]), length)
    return jnp.sum(jnp.where(index < length, value, 0.0))


def place():
    gx, gy = (lax.axis_index(GX), lax.axis_index(GY))
    edge_x = (gx == 0) | (gx == lax.axis_size(GX) - 1)
    edge_y = (gy == 0) | (gy == lax.axis_size(GY) - 1)
    return gx, gy, edge_x, edge_y


def energy_row(field, i, keep_x, keep_y):
    weight = 1.0 - keep_x[i] * keep_y[...]
    value = field[i + H, :, INSIDE, :]
    return weight * (value[0] * value[0] + value[1] * value[1])


def note_energy(seen, step, summed, norm):
    at = STEPS + step
    seen[at : at + 1, :] = jnp.sum(summed, axis=0, keepdims=True) / norm[...]


def note_traces(field, seen, step, table):
    lane = lax.broadcasted_iota(jnp.int32, (1, LANES), 1)

    def sample(n, carry):
        code = table[RECEIVERS + n]
        r, z, ly, lx = (code & 63, (code >> 6) & 255, (code >> 14) & 31, code >> 19)
        line = field[lx + H, z >> 7, pl.ds(ly + LO, 1), :]
        turned = pltpu.roll(line, (r - (z & 127)) & 127, axis=1)
        seen[step : step + 1, :] = jnp.where(lane == r, turned, seen[step : step + 1, :])
        return carry

    lax.fori_loop(0, table[0], sample, 0)


def fetch(pairs, sems):
    copies = []
    for n, (source, target) in enumerate(pairs):
        for c in range(CHUNKS):
            rows = pl.ds(c * (CX // CHUNKS), CX // CHUNKS)
            copies.append(pltpu.make_async_copy(source.at[rows], target.at[rows], sems.at[n, c]))
    for copy in copies:
        copy.start()
    return copies


def split_strips(field, mine_x, mine_y, near_x, far_y, far_x, near_y):
    rows = [field[CX : CX + H, :, INSIDE, :], field[H : 2 * H, :, INSIDE, :]]
    near_x[...] = jnp.where(mine_x, rows[1], rows[0])
    far_x[...] = jnp.where(mine_x, rows[0], rows[1])
    high, low = (LO + CY - H, LO)
    columns = [field[H : H + CX, :, at : at + H, :] for at in (high, low)]
    near_y[...] = jnp.where(mine_y, columns[1], columns[0])
    far_y[...] = jnp.where(mine_y, columns[0], columns[1])


def odd():
    return lax.axis_index(GX) % 2 == 1, lax.axis_index(GY) % 2 == 1


def pack_kernel(pressure, field, near_x, far_y, far_x, near_y, staged, sems):
    copies = fetch([(pressure, staged)], sems)
    field[...] = jnp.zeros(FIELD, jnp.float32)
    for copy in copies:
        copy.wait()
    for half in range(2):
        part = staged[:, :, half * LANES : (half + 1) * LANES]
        field[H : H + CX, half, INSIDE, :] = part
    split_strips(field, *odd(), near_x, far_y, far_x, near_y)


def begin_kernel(
    widths_far, sx_far, sy_far, sz_far, rx_far, ry_far, rz_far, amp_far, old, speed_term,
    field, speed, memory_x, memory_y, zeta_x, zeta_y, seen, keep_x, keep_y, norm, table, amps,
    raw_old, raw_speed, sems, widths_ref, sx, sy, sz, rx, ry, rz, amp, small_sems,
):
    far = (widths_far, sx_far, sy_far, sz_far, rx_far, ry_far, rz_far, amp_far)
    near = (widths_ref, sx, sy, sz, rx, ry, rz, amp)
    small = [
        pltpu.make_async_copy(source, target, small_sems.at[n])
        for n, (source, target) in enumerate(zip(far, near))
    ]
    for copy in small:
        copy.start()
    copies = fetch([(old, raw_old), (speed_term, raw_speed)], sems)
    gx, gy, edge_x, edge_y = place()
    start_x, start_y = (gx * CX, gy * CY)
    seen[...] = jnp.zeros(SEEN, jnp.float32)
    field[...] = jnp.zeros(FIELD, jnp.float32)

    @pl.when(edge_x)
    def _():
        memory_x[...] = jnp.zeros(MEM_X, jnp.float32)
        zeta_x[...] = jnp.zeros(BLOCK, jnp.float32)

    @pl.when(edge_y)
    def _():
        memory_y[...] = jnp.zeros(MEM_Y, jnp.float32)
        zeta_y[...] = jnp.zeros(BLOCK, jnp.float32)

    for copy in small:
        copy.wait()

    @pl.when(edge_x | edge_y)
    def _():
        widths = [widths_ref[n].astype(jnp.float32) for n in range(4)]
        keep = keep_of(widths[:2], start_x, KEEP_Y, 0, NX)
        for i in range(CX):
            keep_x[i] = jnp.broadcast_to(keep[i : i + 1], KEEP_Y)
        keep_y[...] = keep_of(widths[2:], start_y, KEEP_Y, 0, NY)
        cells = float(NX * NY) - whole_sum(widths[:2], NX) * whole_sum(widths[2:], NY)
        norm[...] = wide(float(NZ) * cells)

    def owned(px, py):
        lx, ly = (px - start_x, py - start_y)
        return lx, ly, (lx >= 0) & (lx < CX) & (ly >= 0) & (ly < CY)

    def note(at, n, px, py, pz):
        def add(r, count):
            lx, ly, here = owned(px[r], py[r])
            table[at + count] = (((lx << 5) + ly) << 14) + (pz[r] << 6) + r
            return count + here.astype(jnp.int32)

        return lax.fori_loop(0, n, add, 0, unroll=4)

    table[0] = note(RECEIVERS, NREC, rx, ry, rz)
    table[1] = note(4, NSRC, sx, sy, sz)
    for t in range(STEPS):
        for n in range(NSRC):
            amps[t * NSRC + n] = amp[n, t]
    for copy in copies:
        copy.wait()
    for half in range(2):
        lanes = slice(half * LANES, (half + 1) * LANES)
        field[H : H + CX, half, INSIDE, :] = raw_old[:, :, lanes]
        speed[:, half, :, :] = raw_speed[:, :, lanes]


def inner_kernel(
    step, table, amps, band, current, speed, keep_x, keep_y, norm,
    previous, memory_x_in, memory_y_in, zeta_x_in, zeta_y_in, seen_in,
    following, memory_x, memory_y, zeta_x, zeta_y, seen, bend_z,
):
    _, _, edge_x, edge_y = place()
    halves = [current[H : H + CX, h, INSIDE, :].reshape(CX * CY, LANES) for h in range(2)]
    whole = jnp.concatenate(halves, axis=1)
    high = whole.astype(jnp.bfloat16)
    low = (whole - high.astype(jnp.float32)).astype(jnp.bfloat16)
    bent = jnp.dot(
        jnp.concatenate([high, low], axis=1), band[...], preferred_element_type=jnp.float32
    )
    for h in range(2):
        bend_z[:, h, :, :] = bent[:, h * LANES : (h + 1) * LANES].reshape(CX, CY, LANES)
    source, target = (step % 2, 1 - step % 2)

    def taps(pick, want_first):
        second, first = (0.0, 0.0)
        for k in range(1, 5):
            up, down = (pick(k), pick(-k))
            second = second + second_coef[k - 1] * (up + down)
            if want_first:
                first = first + first_coef[k - 1] * (up - down)
        return second, first

    def first_only(pick):
        total = 0.0
        for k in range(1, 5):
            total = total + first_coef[k - 1] * (pick(k) - pick(-k))
        return total

    def row(in_x, in_y, damped, i, energy):
        for h in range(2):
            centre = current[i + H, h, INSIDE, :]
            second_x, grad_x = taps(lambda k: current[i + H + k, h, INSIDE, :], in_x)
            second_y, grad_y = taps(lambda k: current[i + H, h, LO + k : LO + CY + k, :], in_y)
            laplace = second_x + second_y + (3.0 * centre_coef) * centre
            laplace = laplace + bend_z[i, h] * (1.0 / COMMON)
            if in_x:
                keep = keep_x[i]
                take = keep - 1.0
                flux = first_only(lambda k: memory_x_in[source, i + H + k, h])
                bend = second_x + centre_coef * centre + flux
                zeta = keep * zeta_x_in[i, h] + take * bend
                zeta_x[i, h] = zeta
                laplace = laplace + (flux + zeta)
                memory_x[target, i + H, h] = keep * memory_x_in[source, i + H, h] + take * grad_x
            if in_y:
                keep = keep_y[...]
                take = keep - 1.0
                flux = first_only(lambda k: memory_y_in[i, h, LO + k : LO + CY + k, :])
                bend = second_y + centre_coef * centre + flux
                zeta = keep * zeta_y_in[i, h] + take * bend
                zeta_y[i, h] = zeta
                laplace = laplace + (flux + zeta)
                kept = keep * memory_y_in[i, h, INSIDE, :] + take * grad_y
                memory_y[i, h, INSIDE, :] = kept
            value = 2.0 * centre - previous[i + H, h, INSIDE, :]
            following[i + H, h, INSIDE, :] = value + speed[i, h] * laplace
            if step > 0 and damped:
                energy = energy + (1.0 - keep_x[i] * keep_y[...]) * (centre * centre)
        return energy

    for is_x in (False, True):
        for is_y in (False, True):

            @pl.when((edge_x == is_x) & (edge_y == is_y))
            def _():
                damped = is_x or is_y
                energy = jnp.zeros((CY, LANES), jnp.float32) if damped else 0
                body = functools.partial(row, is_x, is_y, damped)
                if is_x:
                    starts_low = lax.axis_index(GX) == 0
                    first = jnp.where(starts_low, 0, H)
                    energy = lax.fori_loop(first, first + CX - H, body, energy)
                    rest = jnp.where(starts_low, CX - H, 0)
                    body = functools.partial(row, False, is_y, damped)
                    energy = lax.fori_loop(rest, rest + H, body, energy)
                else:
                    energy = lax.fori_loop(0, CX, body, energy, unroll=2)
                if step > 0 and damped:
                    note_energy(seen, step - 1, energy, norm)

    lane = lax.broadcasted_iota(jnp.int32, (1, LANES), 1)

    def inject(n, carry):
        code = table[4 + n]
        s, z, ly, lx = (code & 63, (code >> 6) & 255, (code >> 14) & 31, code >> 19)
        at = (lx + H, z >> 7, pl.ds(ly + LO, 1), slice(None))
        following[at] = following[at] + jnp.where(lane == (z & 127), amps[step * NSRC + s], 0.0)
        return carry

    lax.fori_loop(0, table[1], inject, 0)
    if step > 0:
        note_traces(current, seen, step - 1, table)


def join_kernel(last, *refs):
    if last:
        table, keep_x, keep_y, norm, speed, near_x, far_y, far_x, near_y, _, _ = refs[:11]
        field, seen, beside = refs[11:]
    else:
        speed, near_x, far_y, far_x, near_y, _, field = refs[:7]
        strips, beside = (refs[7:11], refs[11])
    gx, gy, edge_x, edge_y = place()
    mine_x, mine_y = odd()
    halo_x = [jnp.where(mine_x, near_x[...], far_x[...]), jnp.where(mine_x, far_x[...], near_x[...])]
    has = [
        (gx > 0).astype(jnp.float32),
        (gx < lax.axis_size(GX) - 1).astype(jnp.float32),
        (gy > 0).astype(jnp.float32),
        (gy < lax.axis_size(GY) - 1).astype(jnp.float32),
    ]
    low_x, high_x, low_y, high_y = [[e * m for e in second_coef] for m in has]
    beside[:, :, 4:8, :] = jnp.where(mine_y, near_y[...], far_y[...])
    beside[:, :, 8:16, :] = jnp.zeros((CX, 2, 8, LANES), jnp.float32)
    beside[:, :, 16:20, :] = jnp.where(mine_y, far_y[...], near_y[...])

    def ends(i):
        first, final = (0.0, 0.0)
        for k in range(1, 5):
            first = first + low_y[k - 1] * beside[i, :, 8 - k : 16 - k, :]
            final = final + high_y[k - 1] * beside[i, :, 8 + k : 16 + k, :]
        return first, final

    def inside(i, carry):
        first, final = ends(i)
        for at, extra in ((0, first), (16, final)):
            rows = slice(LO + at, LO + at + 8)
            field[i + H, :, rows, :] = (
                field[i + H, :, rows, :] + speed[i, :, at : at + 8, :] * extra
            )
        return carry

    lax.fori_loop(H, CX - H, inside, 0, unroll=4)
    for r in range(H):
        for i, coef, halo in ((r, low_x, halo_x[0]), (CX - H + r, high_x, halo_x[1])):
            across = 0.0
            for k in range(1, 5):
                at = H + i - k if i < H else i + k - CX
                if 0 <= at < H:
                    across = across + coef[k - 1] * halo[at]
            first, final = ends(i)
            for at, extra in ((0, first), (8, None), (16, final)):
                rows = slice(LO + at, LO + at + 8)
                part = across[:, at : at + 8, :]
                part = part if extra is None else part + extra
                field[i + H, :, rows, :] = (
                    field[i + H, :, rows, :] + speed[i, :, at : at + 8, :] * part
                )
    if not last:
        split_strips(field, mine_x, mine_y, *strips)
        return

    @pl.when(edge_x | edge_y)
    def _():
        add = lambda i, summed: summed + energy_row(field, i, keep_x, keep_y)
        zero = jnp.zeros((CY, LANES), jnp.float32)
        note_energy(seen, STEPS - 1, lax.fori_loop(0, CX, add, zero, unroll=4), norm)

    note_traces(field, seen, STEPS - 1, table)


def finish_kernel(field, pressure):
    for half in range(2):
        part = field[H : H + CX, half, INSIDE, :]
        pressure[:, :, half * LANES : (half + 1) * LANES] = part


def report_kernel(*refs):
    parts, (traces, energy) = (refs[:-2], refs[-2:])
    seen = parts[0][...]
    for part in parts[1:]:
        seen = seen + part[...]
    traces[...] = seen[:STEPS, :NREC]
    energy[...] = jnp.sum(seen[STEPS:].T, axis=0)


def vmem(count):
    return [pl.BlockSpec(memory_space=pltpu.VMEM)] * count


def smem(count):
    return [pl.BlockSpec(memory_space=pltpu.SMEM)] * count


def hbm(count):
    return [pl.BlockSpec(memory_space=pltpu.HBM)] * count


def shape(*sizes):
    return [jax.ShapeDtypeStruct(size, jnp.float32) for size in sizes]


def limit(mebibytes):
    return pltpu.CompilerParams(vmem_limit_bytes=mebibytes * 1024 * 1024)


def swap(strip, axis, far):
    rows, columns = (lax.axis_size(GX), lax.axis_size(GY))
    pairs = []
    for gx in range(rows):
        for gy in range(columns):
            to_x = ((gx + far) ^ 1) - far if axis == GX else gx
            to_y = ((gy + far) ^ 1) - far if axis == GY else gy
            if not 0 <= to_x < rows:
                to_x, to_y = (gx, gy ^ 1)
            if not 0 <= to_y < columns:
                to_x, to_y = (gx ^ 1, gy)
            pairs.append((gx * columns + gy, to_x * columns + to_y))
    return lax.ppermute(strip, BOTH, pairs)


def exchange(strips):
    near_x, far_y, far_x, near_y = strips
    return (swap(near_x, GX, 0), swap(far_y, GY, 1), swap(far_x, GX, 1), swap(near_y, GY, 0))


def spread(value, by):
    columns = lax.axis_size(GY)
    pairs = []
    for gx in range(lax.axis_size(GX)):
        for gy in range(columns):
            pairs.append((gx * columns + gy, (gx ^ by[0]) * columns + (gy ^ by[1])))
    return lax.ppermute(value, BOTH, pairs)


def gather_sums(value):
    if (lax.axis_size(GX), lax.axis_size(GY)) != (8, 16):
        return [lax.psum(value, BOTH)]
    parts = [value, spread(value, (0, 1))]
    for flips in (((1, 0), (0, 2), (1, 2)), ((0, 4), (0, 8), (0, 12)), ((2, 0), (4, 0), (6, 0))):
        value = functools.reduce(jnp.add, parts)
        parts = [value] + [spread(value, by) for by in flips]
    return parts


def per_device(
    pressure,
    pressure_old,
    speed_term,
    layer_width,
    source_x,
    source_y,
    source_z,
    source_amp,
    receiver_x,
    receiver_y,
    receiver_z,
):
    stay = lambda value: pltpu.with_memory_space_constraint(value, pltpu.HBM)
    pressure, pressure_old, speed_term = [stay(v) for v in (pressure, pressure_old, speed_term)]
    small = [layer_width, source_x, source_y, source_z, receiver_x, receiver_y, receiver_z, source_amp.T]
    small = [stay(v) for v in small]
    staged = pltpu.VMEM(pressure.shape, jnp.float32)
    strips_out = shape(STRIP_X, STRIP_Y, STRIP_X, STRIP_Y)
    current, *strips = pl.pallas_call(
        pack_kernel,
        out_shape=shape(FIELD) + strips_out,
        in_specs=hbm(1),
        out_specs=vmem(5),
        scratch_shapes=[staged, pltpu.SemaphoreType.DMA((1, CHUNKS))],
        compiler_params=limit(8),
    )(pressure)
    previous, speed, *rest = pl.pallas_call(
        begin_kernel,
        out_shape=shape(FIELD, BLOCK, MEM_X, MEM_Y, BLOCK, BLOCK, SEEN, KEEP_X, KEEP_Y, NORM)
        + [
            jax.ShapeDtypeStruct((TABLE,), jnp.int32),
            jax.ShapeDtypeStruct((STEPS * NSRC,), jnp.float32),
        ],
        in_specs=hbm(10),
        out_specs=vmem(10) + smem(2),
        scratch_shapes=[staged, staged, pltpu.SemaphoreType.DMA((2, CHUNKS))]
        + [pltpu.SMEM((n,), jnp.int32) for n in (4, NSRC, NSRC, NSRC, NREC, NREC, NREC)]
        + [pltpu.SMEM((NSRC, STEPS), jnp.float32), pltpu.SemaphoreType.DMA((8,))],
        compiler_params=limit(8),
    )(*small, pressure_old, speed_term)
    state, keeps, table, amps = (rest[:5], rest[5:8], rest[8], rest[9])
    band = jnp.asarray(band_matrix())
    beside = pltpu.VMEM((CX, 2, 24, LANES), jnp.float32)
    for step in range(STEPS):
        halos = exchange(strips)
        following, *state = pl.pallas_call(
            functools.partial(inner_kernel, step),
            out_shape=shape(FIELD, MEM_X, MEM_Y, BLOCK, BLOCK, SEEN),
            in_specs=smem(2) + vmem(12),
            out_specs=vmem(6),
            scratch_shapes=[pltpu.VMEM(BLOCK, jnp.float32)],
            input_output_aliases={8: 0, 9: 1, 10: 2, 11: 3, 12: 4, 13: 5},
            compiler_params=limit(8),
        )(table, amps, band, current, speed, *keeps, previous, *state)
        previous = current
        if step < STEPS - 1:
            current, *strips = pl.pallas_call(
                functools.partial(join_kernel, False),
                out_shape=shape(FIELD) + strips_out,
                in_specs=vmem(6),
                out_specs=vmem(5),
                scratch_shapes=[beside],
                input_output_aliases={5: 0},
                compiler_params=limit(4),
            )(speed, *halos, following)
        else:
            current, seen = pl.pallas_call(
                functools.partial(join_kernel, True),
                out_shape=shape(FIELD, SEEN),
                in_specs=smem(1) + vmem(10),
                out_specs=vmem(2),
                scratch_shapes=[beside],
                input_output_aliases={9: 0, 10: 1},
                compiler_params=limit(4),
            )(table, *keeps, speed, *halos, following, state[-1])
    final = pl.pallas_call(
        finish_kernel,
        out_shape=jax.ShapeDtypeStruct(pressure.shape, jnp.float32),
        in_specs=vmem(1),
        out_specs=pl.BlockSpec(memory_space=pltpu.VMEM),
        compiler_params=limit(4),
    )(current)
    parts = gather_sums(seen)
    traces, energy = pl.pallas_call(
        report_kernel,
        out_shape=shape((STEPS, NREC), (STEPS,)),
        in_specs=vmem(len(parts)),
        out_specs=vmem(2),
        compiler_params=limit(2),
    )(*parts)
    return final, traces.T, energy


def solution(mesh):
    block = P(GX, GY, None)
    return jax.shard_map(
        per_device,
        mesh=mesh,
        in_specs=(block, block, block) + (P(),) * 8,
        out_specs=(block, P(), P()),
        check_vma=False,
    )
```
